1024 devices in a mesh: rows: 64 (over z_lo, x), filt: 16 (over y, z_hi, core).
Axes of the slice: x: 4, y: 4, z: 32 (z_hi: 2, z_lo: 16; z = z_hi * 16 + z_lo), core: 2. Of those that a mesh axis runs over, the one named last changes fastest.
Arguments:
- features: bfloat16 [768, 48, 2048], P('rows'), may hold values from -6 to 6
- point_weight: bfloat16 [2048, 256], P(None, 'filt'), may hold values from -0.125 to 0.125
- dilated_weight: bfloat16 [3, 3, 3, 2048, 256], P(None, None, None, None, 'filt'), may hold values from -0.046875 to 0.046875
- branch_bias: float32 [4, 256], P(None, 'filt'), may hold values from -3 to 3
- project_weight: bfloat16 [4, 256, 256], replicated, may hold values from -0.1875 to 0.1875
- project_bias: float32 [256], replicated, may hold values from -3 to 3
- cotangent: bfloat16 [768, 48, 256], P('rows'), may hold values from -6 to 6
Outputs:
- head_output: bfloat16 [768, 48, 256], P('rows', None, 'filt')
- feature_grad: bfloat16 [768, 48, 2048], P('rows', None, 'filt')
The draws below stay inside these ranges and needn't reach their ends.
All inputs are finite; a program needn't handle non-finite values.
Results may differ from the reference program's by a relative error of at most 0.035.
The reference program's roundings to bfloat16 on the way count: a program that leaves them out, or rounds other values in their place, can miss the bound.
Values may be sent and summed in bfloat16 or wider, within the bound.
A program may use at most 128 MiB of HBM per device.

```python
import jax
import jax.numpy as jnp
from jax import lax

C = 2048
BR = 256
OUTC = 256
FIRST_DILATION = 12
SECOND_DILATION = 24
THIRD_DILATION = 36
COLS = 48
ROWS = 768


def steps_of(rng, shape, split, least, top_value):
    gain = 1.0
    for dim, parts in split:
        steps = jax.random.uniform(jax.random.fold_in(jax.random.fold_in(rng, 6), dim), (parts,), jnp.float32, least / len(split), top_value / len(split))
        gain = gain * jnp.repeat(jnp.exp(steps), shape[dim] // parts).reshape((-1,) + (1,) * (len(shape) - 1 - dim))
    return gain


def centred(stream_key, shape, width, bound, pieces=(), dtype=jnp.bfloat16):
    level = steps_of(stream_key, shape, pieces, -0.22, 0.18) if pieces else 1.0
    drawn = jax.random.normal(stream_key, shape, jnp.float32) * width * level
    return jnp.minimum(jnp.maximum(drawn, -bound), bound).astype(dtype)


def setup_inputs(seed: int = 0) -> dict:
    streams_of = jax.random.split(jax.random.key(seed), 8)
    features = centred(streams_of[0], (ROWS, COLS, C), 1.0, 6.0, ((0, 64),))
    point_weight = centred(streams_of[1], (C, BR), C ** -0.5, 0.125, ((1, 16),))
    dilated_weight = centred(streams_of[2], (3, 3, 3, C, BR), (9 * C) ** -0.5, 0.046875, ((4, 16),))
    branch_bias = centred(streams_of[3], (4, BR), 0.5, 3.0, ((1, 16),), jnp.float32)
    project_weight = centred(streams_of[4], (4, BR, OUTC), (4 * BR) ** -0.5, 0.1875)
    project_bias = centred(streams_of[5], (OUTC,), 0.5, 3.0, (), jnp.float32)
    cotangent = centred(streams_of[6], (ROWS, COLS, OUTC), 1.0, 6.0, ((0, 64),))
    return dict(features=features, point_weight=point_weight, dilated_weight=dilated_weight, branch_bias=branch_bias, project_weight=project_weight, project_bias=project_bias, cotangent=cotangent)


def shift_axis(field, axis_index, amount):
    extent = field.shape[axis_index]
    if amount == 0:
        return field
    if abs(amount) >= extent:
        return jnp.zeros_like(field)
    padding = [(0, 0)] * field.ndim
    if amount > 0:
        kept = lax.slice_in_dim(field, amount, extent, axis=axis_index)
        padding[axis_index] = (0, amount)
    else:
        kept = lax.slice_in_dim(field, 0, extent + amount, axis=axis_index)
        padding[axis_index] = (-amount, 0)
    return jnp.pad(kept, padding)


def shift_field(field, rows_by, cols_by):
    return shift_axis(shift_axis(field, 0, rows_by), 1, cols_by)


def reference(features, point_weight, dilated_weight, branch_bias, project_weight, project_bias, cotangent):
    flattened = features.reshape(ROWS * COLS, C)
    dilation_rates = (FIRST_DILATION, SECOND_DILATION, THIRD_DILATION)
    point_pre = jnp.dot(flattened, point_weight, preferred_element_type=jnp.float32).reshape(ROWS, COLS, BR)
    pre_list = [point_pre + branch_bias[0]]
    for branch, dilation in enumerate(dilation_rates):
        summed_result = jnp.zeros((ROWS, COLS, BR), jnp.float32)
        for row_tap in range(3):
            for col_tap in range(3):
                product = jnp.dot(flattened, dilated_weight[branch, row_tap, col_tap], preferred_element_type=jnp.float32)
                product = product.reshape(ROWS, COLS, BR)
                summed_result = summed_result + shift_field(product, (row_tap - 1) * dilation, (col_tap - 1) * dilation)
        pre_list.append(summed_result + branch_bias[branch + 1])
    project_pre = jnp.zeros((ROWS * COLS, OUTC), jnp.float32) + project_bias
    for branch in range(4):
        activation = jnp.maximum(pre_list[branch], 0.0).astype(jnp.bfloat16).reshape(ROWS * COLS, BR)
        project_pre = project_pre + jnp.dot(activation, project_weight[branch], preferred_element_type=jnp.float32)
    head_output = jnp.maximum(project_pre, 0.0).astype(jnp.bfloat16).reshape(ROWS, COLS, OUTC)
    head_grad = jnp.where(project_pre > 0, cotangent.reshape(ROWS * COLS, OUTC).astype(jnp.float32), 0.0).astype(jnp.bfloat16)
    input_grad = jnp.zeros((ROWS * COLS, C), jnp.float32)
    for branch in range(4):
        act_grad = jnp.dot(head_grad, project_weight[branch].T, preferred_element_type=jnp.float32).reshape(ROWS, COLS, BR)
        branch_grad = jnp.where(pre_list[branch] > 0, act_grad, 0.0).astype(jnp.bfloat16)
        if branch == 0:
            input_grad = input_grad + jnp.dot(branch_grad.reshape(ROWS * COLS, BR), point_weight.T, preferred_element_type=jnp.float32)
        else:
            dilation = dilation_rates[branch - 1]
            for row_tap in range(3):
                for col_tap in range(3):
                    moved = shift_field(branch_grad, -(row_tap - 1) * dilation, -(col_tap - 1) * dilation)
                    input_grad = input_grad + jnp.dot(moved.reshape(ROWS * COLS, BR), dilated_weight[branch - 1, row_tap, col_tap].T, preferred_element_type=jnp.float32)
    feature_grad = input_grad.astype(jnp.bfloat16).reshape(ROWS, COLS, C)
    return head_output, feature_grad
```

```python
import jax
import jax.numpy as jnp
from jax import lax
from jax.experimental import pallas as pl
from jax.experimental.pallas import tpu as pltpu
from jax.sharding import PartitionSpec as P

FIRST_DILATION = 12
SECOND_DILATION = 24
THIRD_DILATION = 36
DILATIONS = (FIRST_DILATION, SECOND_DILATION, THIRD_DILATION)
ROW_BLOCKS = 64
HEIGHT = 12
BREADTH = 48
PIXELS = HEIGHT * BREADTH
LANES = 640
CHANNELS = 2048
OWN = 16
TAPS = 28
TERMS = TAPS * OWN
MEMBERS = 16
OUTPUTS = 256
BLOCK = 128
PIECE_ROWS = TERMS // 4
PIECE_LANES = 256
MESH = pl.DeviceIdType.MESH
BF16 = jnp.bfloat16
F32 = jnp.float32


def device(x, y, z, core):
    x, y, z = lax.rem(x + 4, 4), lax.rem(y + 4, 4), lax.rem(z + 32, 32)
    return (lax.rem(z, 16) * 4 + x, (y * 2 + z // 16) * 2 + core)


def remote(source, target, send_sem, recv_sem, where):
    return pltpu.make_async_remote_copy(
        src_ref=source,
        dst_ref=target,
        send_sem=send_sem,
        recv_sem=recv_sem,
        device_id=where,
        device_id_type=MESH,
    )


def kernel(
    x_hbm, dilated_hbm, point_hbm, project_hbm, cot_hbm, bias_hbm, project_bias_hbm,
    head_ref, grad_ref,
    bias_ref, project_bias_ref, x_buf, w_buf, w_both, project, project_t, cot_buf, cot_t, columns,
    taps, row_send, row_recv, acts, pre, grads, grad_recv, spread, spread_t,
    part, part_low, core_recv, sum_send, sum_recv,
    load_sem, fill_sem, row_ss, row_rs, act_ss, act_rs, first_ss, first_rs, zg_ss, zg_rs,
    xg_ss, xg_rs, grow_ss, grow_rs, core_ss, core_rs, sum_ss, sum_rs,
):
    row = lax.axis_index("rows")
    member = lax.axis_index("filt")
    x, z_low = lax.rem(row, 4), row // 4
    y, half, core = member // 4, lax.rem(member // 2, 2), lax.rem(member, 2)
    z = half * 16 + z_low
    z_quarter = lax.rem(z_low, 4)
    other = member + 2 - 4 * half
    twin = 1 - 2 * core

    def row_offset(slot):
        return (slot // 2 + 1) * (1 - 2 * (slot % 2))

    def sends(slot):
        place = row + row_offset(slot)
        return jnp.logical_and(place >= 0, place < ROW_BLOCKS)

    def gets(slot):
        place = row - row_offset(slot)
        return jnp.logical_and(place >= 0, place < ROW_BLOCKS)

    opposite = device(x, y, z + 16, core)
    eighth = device(x, y, z + jnp.where(z_low >= 8, 8, -8), core)
    partner = device(x, y, z, 1 - core)
    y_peers = [device(x, y + d, z, core) for d in (1, 3, 2)]
    y_members = [(lax.rem(y + d, 4) * 2 + half) * 2 + core for d in (1, 3, 2)]
    y_others = [(lax.rem(y + d, 4) * 2 + 1 - half) * 2 + core for d in (1, 3, 2)]
    z_base = z - z_quarter
    z_peers = [device(x, y, z_base + lax.rem(z_quarter + d, 4), core) for d in (1, 2, 3)]
    x_peers = [device(x + d, y, z, core) for d in (1, 2, 3)]

    barrier = pltpu.get_barrier_semaphore()
    fixed_peers = [opposite, eighth, partner] + y_peers + z_peers + x_peers
    for peer in fixed_peers:
        pl.semaphore_signal(barrier, inc=1, device_id=peer, device_id_type=MESH)
    heard = jnp.int32(len(fixed_peers))
    for slot in range(6):
        @pl.when(sends(slot))
        def _():
            pl.semaphore_signal(
                barrier, inc=1, device_id=(row + row_offset(slot), member), device_id_type=MESH
            )
        heard = heard + sends(slot).astype(jnp.int32)

    loads = [
        pltpu.make_async_copy(x_hbm, x_buf.at[pl.ds(0, PIXELS)], load_sem.at[0]),
        pltpu.make_async_copy(dilated_hbm, w_buf.at[pl.ds(0, TERMS - OWN)], load_sem.at[1]),
        pltpu.make_async_copy(point_hbm, w_buf.at[pl.ds(TERMS - OWN, OWN)], load_sem.at[2]),
        pltpu.make_async_copy(cot_hbm, cot_buf.at[pl.ds(0, PIXELS)], load_sem.at[3]),
    ] + [
        pltpu.make_async_copy(project_hbm.at[k], project.at[:, k], load_sem.at[4 + k])
        for k in range(4)
    ] + [
        pltpu.make_async_copy(bias_hbm, bias_ref, load_sem.at[8]),
        pltpu.make_async_copy(project_bias_hbm, project_bias_ref, load_sem.at[9]),
    ]
    for load in loads:
        load.start()
    x_buf[pl.ds(PIXELS, LANES - PIXELS), :] = jnp.zeros((LANES - PIXELS, CHANNELS), BF16)
    cot_buf[pl.ds(PIXELS, LANES - PIXELS), :] = jnp.zeros((LANES - PIXELS, OUTPUTS), BF16)
    for load in loads[:3]:
        load.wait()

    own_fill = []
    for block in range(4):
        lanes = pl.multiple_of(block * 512 + half * 256, 256)
        own_fill.append(
            pltpu.make_async_copy(
                w_buf.at[:, pl.ds(lanes, 256)],
                w_both.at[pl.ds(0, TERMS), pl.ds(block * 256, 256)],
                fill_sem.at[block],
            )
        )
    for fill in own_fill:
        fill.start()

    taps[...] = lax.dot_general(
        w_buf[...], x_buf[...], (((1,), (1,)), ((), ())), preferred_element_type=F32
    )

    column = lax.rem(lax.broadcasted_iota(jnp.int32, (1, LANES), 1), BREADTH)

    def shift_columns(field, amount):
        if amount == 0:
            return field
        inside = jnp.logical_and(column + amount >= 0, column + amount < BREADTH)
        return jnp.where(inside, pltpu.roll(field, (-amount) % LANES, 1), 0.0)

    def tap(k, i, j):
        return taps[pl.ds((9 * k + 3 * i + j) * OWN, OWN), :]

    def row_sum(k, i):
        d = DILATIONS[k]
        return (
            shift_columns(tap(k, i, 0), -d) + tap(k, i, 1) + shift_columns(tap(k, i, 2), d)
        )

    for k in range(3):
        row_send[2 * k] = row_sum(k, 0)
        row_send[2 * k + 1] = row_sum(k, 2)

    pl.semaphore_wait(barrier, heard)

    def row_copy(slot):
        return remote(
            row_send.at[slot], row_recv.at[slot], row_ss.at[slot], row_rs.at[slot],
            (row + row_offset(slot), member),
        )

    for slot in (4, 5, 2, 3, 0, 1):
        @pl.when(sends(slot))
        def _():
            row_copy(slot).start()

    z_rows = pl.multiple_of(z_quarter * PIECE_ROWS, 16)
    far_rows = pl.multiple_of(TERMS + z_quarter * PIECE_ROWS, 16)
    far_lanes = pl.multiple_of(x * PIECE_LANES, 128)
    give_lanes = pl.multiple_of(x * 512 + (1 - half) * 256, 256)
    first = remote(
        w_buf.at[pl.ds(z_rows, PIECE_ROWS), pl.ds(give_lanes, PIECE_LANES)],
        w_both.at[pl.ds(far_rows, PIECE_ROWS), pl.ds(far_lanes, PIECE_LANES)],
        first_ss.at[0], first_rs.at[0], eighth,
    )
    first.start()

    def diagonal(values, size):
        same = lax.broadcasted_iota(jnp.int32, (size, size), 0) == lax.broadcasted_iota(
            jnp.int32, (size, size), 1
        )
        return jnp.sum(
            jnp.where(same, jnp.broadcast_to(values, (size, size)), 0.0), axis=1, keepdims=True
        )

    for load in loads[8:]:
        load.wait()
    bias = bias_ref[...]
    biases = [diagonal(bias[k:k + 1, :], OWN) for k in range(4)]
    acts[member, pl.ds(0, OWN), :] = jnp.maximum(
        taps[pl.ds(TERMS - OWN, OWN), :] + biases[0], 0.0
    ).astype(BF16)
    centres = [row_sum(k, 1) + biases[k + 1] for k in range(3)]

    for k in range(3):
        total = centres[k]
        for slot in (2 * k, 2 * k + 1):
            @pl.when(gets(slot))
            def _():
                row_copy(slot).wait_recv()
            total = total + jnp.where(gets(slot), row_recv[slot], 0.0)
        acts[member, pl.ds((k + 1) * OWN, OWN), :] = jnp.maximum(total, 0.0).astype(BF16)

    started = []

    def pass_block(block, where):
        n = len(started)
        copy = remote(acts.at[block], acts.at[block], act_ss.at[n], act_rs.at[block], where)
        copy.start()
        started.append(copy)

    def await_block(block):
        remote(acts.at[block], acts.at[block], act_ss.at[0], act_rs.at[block], partner).wait_recv()

    pass_block(member, opposite)
    for peer in y_peers:
        pass_block(member, peer)
    pass_block(member, partner)

    for load in loads[3:8]:
        load.wait()
    project_rows = project[...].reshape(MEMBERS * 4 * OWN, OUTPUTS)
    project_t[...] = project_rows.T
    cot_t[...] = cot_buf[...].astype(F32).T
    columns[...] = jnp.broadcast_to(diagonal(project_bias_ref[...], OUTPUTS), (OUTPUTS, BLOCK))

    for n in range(3):
        await_block(y_members[n])
        pass_block(y_members[n], partner)

    def z_copy(d):
        return remote(
            w_both.at[pl.ds(far_rows, PIECE_ROWS), pl.ds(far_lanes, PIECE_LANES)],
            w_both.at[pl.ds(far_rows, PIECE_ROWS), pl.ds(far_lanes, PIECE_LANES)],
            zg_ss.at[d - 1], zg_rs.at[d - 1], z_peers[d - 1],
        )

    def x_copy(d, e):
        rows_from = pl.multiple_of(
            TERMS + lax.rem(z_quarter + 4 - d, 4) * PIECE_ROWS, 16
        )
        return remote(
            w_both.at[pl.ds(rows_from, PIECE_ROWS), pl.ds(far_lanes, PIECE_LANES)],
            w_both.at[pl.ds(rows_from, PIECE_ROWS), pl.ds(far_lanes, PIECE_LANES)],
            xg_ss.at[3 * d + e - 1], xg_rs.at[3 * d + e - 1], x_peers[e - 1],
        )

    first.wait_recv()
    for d in (1, 2, 3):
        z_copy(d).start()
    for e in (1, 2, 3):
        x_copy(0, e).start()

    await_block(other)
    for peer in y_peers:
        pass_block(other, peer)
    pass_block(other, partner)

    for d in (1, 2, 3):
        z_copy(d).wait_recv()
        for e in (1, 2, 3):
            x_copy(d, e).start()

    for n in range(3):
        await_block(y_others[n])
        pass_block(y_others[n], partner)
    for block in [member, other] + y_members + y_others:
        await_block(block + twin)

    pre[...] = (
        jnp.dot(
            project_t[...],
            acts[...].reshape(MEMBERS * 4 * OWN, LANES),
            preferred_element_type=F32,
        )
        + columns[:, 0:1]
    )
    head_grad = jnp.where(pre[...] > 0, cot_t[...], 0.0).astype(BF16)
    for side, block in ((0, member), (1, other)):
        act_grad = jnp.dot(
            project[block].reshape(4 * OWN, OUTPUTS), head_grad, preferred_element_type=F32
        )
        branch_grad = jnp.where(acts[block] > 0, act_grad, 0.0).astype(BF16)
        for k in range(4):
            grads[k, pl.ds(side * OWN, OWN), :] = branch_grad[k * OWN:(k + 1) * OWN]

    def grad_copy(slot):
        return remote(
            grads.at[slot // 2 + 1], grad_recv.at[slot], grow_ss.at[slot], grow_rs.at[slot],
            (row + row_offset(slot), member),
        )

    for slot in (4, 5, 2, 3, 0, 1):
        @pl.when(sends(slot))
        def _():
            grad_copy(slot).start()

    own_head = jnp.maximum(pre[pl.ds(pl.multiple_of(member * OWN, OWN), OWN), :], 0.0)
    for r in range(HEIGHT):
        head_ref[r] = own_head[:, r * BREADTH:(r + 1) * BREADTH].astype(BF16)

    def put(values, t):
        low = values.astype(BF16)
        for side in range(2):
            spread[pl.ds(side * TERMS + t * OWN, OWN), :] = low[side * OWN:(side + 1) * OWN]

    def put_columns(field, k, i):
        for j in range(3):
            put(shift_columns(field, -(j - 1) * DILATIONS[k]), 9 * k + 3 * i + j)

    put(grads[0].astype(F32), TAPS - 1)
    for k in range(3):
        put_columns(grads[k + 1].astype(F32), k, 1)
    for k in range(3):
        for slot, i in ((2 * k, 2), (2 * k + 1, 0)):
            @pl.when(gets(slot))
            def _():
                grad_copy(slot).wait_recv()
            put_columns(jnp.where(gets(slot), grad_recv[slot].astype(F32), 0.0), k, i)

    spread_t[...] = spread[...].T

    for fill in own_fill:
        fill.wait()
    for d in range(4):
        for e in (1, 2, 3):
            x_copy(d, e).wait_recv()

    def core_copy(n):
        return remote(
            part_low.at[n, 1 - core], core_recv.at[n], core_ss.at[n], core_rs.at[n], partner
        )

    order = (2, 1, 3, 0)
    for n, d in enumerate(order):
        lanes = pl.multiple_of(lax.rem(y + d, 4) * 256, 256)
        product = jnp.dot(
            spread_t[pl.ds(0, PIXELS), :], w_both[:, pl.ds(lanes, 256)], preferred_element_type=F32
        )
        for c in range(2):
            piece = product[:, c * BLOCK:(c + 1) * BLOCK]
            part[n, c] = piece
            part_low[n, c] = piece.astype(BF16)
        core_copy(n).start()

    def sum_copy(n):
        return remote(
            sum_send.at[n], sum_recv.at[n], sum_ss.at[n], sum_rs.at[n],
            device(x, y + order[n], z, core),
        )

    for n in range(3):
        core_copy(n).wait_recv()
        sum_send[n] = (part[n, core] + core_recv[n].astype(F32)).astype(BF16)
        sum_copy(n).start()
    core_copy(3).wait_recv()
    total = part[3, core] + core_recv[3].astype(F32)
    for n in range(3):
        sum_copy(n).wait_recv()
        total = total + sum_recv[n].astype(F32)
    grad_ref[...] = total.astype(BF16)

    for slot in range(6):
        @pl.when(sends(slot))
        def _():
            row_copy(slot).wait_send()
            grad_copy(slot).wait_send()
    first.wait_send()
    for copy in started:
        copy.wait_send()
    for d in (1, 2, 3):
        z_copy(d).wait_send()
    for d in range(4):
        for e in (1, 2, 3):
            x_copy(d, e).wait_send()
    for n in range(4):
        core_copy(n).wait_send()
    for n in range(3):
        sum_copy(n).wait_send()


def on_device(
    features, point_weight, dilated_weight, branch_bias, project_weight, project_bias, cotangent
):
    in_place = pl.BlockSpec(memory_space=pltpu.HBM)
    vmem = pl.BlockSpec(memory_space=pltpu.VMEM)
    dma = pltpu.SemaphoreType.DMA
    head, grad = pl.pallas_call(
        kernel,
        out_shape=(
            jax.ShapeDtypeStruct((HEIGHT, OWN, BREADTH), BF16),
            jax.ShapeDtypeStruct((PIXELS, BLOCK), BF16),
        ),
        in_specs=[in_place] * 7,
        out_specs=(vmem, vmem),
        scratch_shapes=[
            pltpu.VMEM((4, OWN), F32),
            pltpu.VMEM((1, OUTPUTS), F32),
            pltpu.VMEM((LANES, CHANNELS), BF16),
            pltpu.VMEM((TERMS, CHANNELS), BF16),
            pltpu.VMEM((2 * TERMS, CHANNELS // 2), BF16),
            pltpu.VMEM((MEMBERS, 4, OWN, OUTPUTS), BF16),
            pltpu.VMEM((OUTPUTS, MEMBERS * 4 * OWN), BF16),
            pltpu.VMEM((LANES, OUTPUTS), BF16),
            pltpu.VMEM((OUTPUTS, LANES), F32),
            pltpu.VMEM((OUTPUTS, BLOCK), F32),
            pltpu.VMEM((TERMS, LANES), F32),
            pltpu.VMEM((6, OWN, LANES), F32),
            pltpu.VMEM((6, OWN, LANES), F32),
            pltpu.VMEM((MEMBERS, 4 * OWN, LANES), BF16),
            pltpu.VMEM((OUTPUTS, LANES), F32),
            pltpu.VMEM((4, 2 * OWN, LANES), BF16),
            pltpu.VMEM((6, 2 * OWN, LANES), BF16),
            pltpu.VMEM((2 * TERMS, LANES), BF16),
            pltpu.VMEM((LANES, 2 * TERMS), BF16),
            pltpu.VMEM((4, 2, PIXELS, BLOCK), F32),
            pltpu.VMEM((4, 2, PIXELS, BLOCK), BF16),
            pltpu.VMEM((4, PIXELS, BLOCK), BF16),
            pltpu.VMEM((3, PIXELS, BLOCK), BF16),
            pltpu.VMEM((3, PIXELS, BLOCK), BF16),
            dma((10,)), dma((4,)), dma((6,)), dma((6,)), dma((15,)), dma((16,)),
            dma((1,)), dma((1,)), dma((3,)), dma((3,)), dma((12,)), dma((12,)),
            dma((6,)), dma((6,)), dma((4,)), dma((4,)), dma((3,)), dma((3,)),
        ],
        compiler_params=pltpu.CompilerParams(
            collective_id=0, has_side_effects=True, vmem_limit_bytes=58 * 1024 * 1024
        ),
        name="pyramid",
    )(
        features.reshape(PIXELS, CHANNELS),
        jnp.transpose(dilated_weight, (0, 1, 2, 4, 3)).reshape(TERMS - OWN, CHANNELS),
        point_weight.T,
        project_weight.reshape(4, MEMBERS, OWN, OUTPUTS),
        cotangent.reshape(PIXELS, OUTPUTS),
        branch_bias,
        project_bias.reshape(1, OUTPUTS),
    )
    return (jnp.transpose(head, (0, 2, 1)), grad.reshape(HEIGHT, BREADTH, BLOCK))


def solution(mesh):
    in_specs = (
        P("rows", None, None),
        P(None, "filt"),
        P(None, None, None, None, "filt"),
        P(None, "filt"),
        P(),
        P(),
        P("rows", None, None),
    )
    out_specs = (P("rows", None, "filt"), P("rows", None, "filt"))
    return jax.shard_map(
        on_device, mesh=mesh, in_specs=in_specs, out_specs=out_specs, check_vma=False
    )
```

```python
import jax
import jax.numpy as jnp
from jax import lax
from jax.experimental import pallas as pl
from jax.experimental.pallas import tpu as pltpu
from jax.sharding import PartitionSpec as P

FIRST_DILATION = 12
SECOND_DILATION = 24
THIRD_DILATION = 36
DILATIONS = (FIRST_DILATION, SECOND_DILATION, THIRD_DILATION)
ROW_BLOCKS = 64
HEIGHT = 12
BREADTH = 48
PIXELS = HEIGHT * BREADTH
LANES = 640
CHANNELS = 2048
OWN = 16
TAPS = 28
TERMS = TAPS * OWN
MEMBERS = 16
OUTPUTS = 256
BLOCK = 128
PIECE_ROWS = TERMS // 4
PIECE_LANES = 256
MESH = pl.DeviceIdType.MESH
BF16 = jnp.bfloat16
F32 = jnp.float32


def device(x, y, z, core):
    x, y, z = lax.rem(x + 4, 4), lax.rem(y + 4, 4), lax.rem(z + 32, 32)
    return (lax.rem(z, 16) * 4 + x, (y * 2 + z // 16) * 2 + core)


def remote(source, target, send_sem, recv_sem, where):
    return pltpu.make_async_remote_copy(
        src_ref=source,
        dst_ref=target,
        send_sem=send_sem,
        recv_sem=recv_sem,
        device_id=where,
        device_id_type=MESH,
    )


def kernel(
    x_hbm, dilated_hbm, point_hbm, project_hbm, cot_hbm, bias_hbm, project_bias_hbm,
    head_ref, grad_ref,
    bias_ref, project_bias_ref, x_buf, w_buf, w_both, project, project_t, cot_buf, cot_t, columns,
    taps, row_send, row_recv, acts, pre, grads, grad_recv, spread, spread_t,
    part_sum, part_low, core_recv, sum_send, sum_recv,
    near, far, load_sem, fill_sem, row_ss, row_rs, act_ss, act_rs, first_ss, first_rs, zg_ss, zg_rs,
    xg_ss, xg_rs, grow_ss, grow_rs, core_ss, core_rs, sum_ss, sum_rs,
):
    row = lax.axis_index("rows")
    member = lax.axis_index("filt")
    x, z_low = lax.rem(row, 4), row // 4
    y, half, core = member // 4, lax.rem(member // 2, 2), lax.rem(member, 2)
    z = half * 16 + z_low
    z_quarter = lax.rem(z_low, 4)
    other = member + 2 - 4 * half
    twin = 1 - 2 * core

    def row_offset(slot):
        return (slot // 2 + 1) * (1 - 2 * (slot % 2))

    def sends(slot):
        place = row + row_offset(slot)
        return jnp.logical_and(place >= 0, place < ROW_BLOCKS)

    def gets(slot):
        place = row - row_offset(slot)
        return jnp.logical_and(place >= 0, place < ROW_BLOCKS)

    opposite = device(x, y, z + 16, core)
    eighth = device(x, y, z + jnp.where(z_low >= 8, 8, -8), core)
    partner = device(x, y, z, 1 - core)
    y_steps = (2, 1, 3)
    z_up, z_down = device(x, y, z + 4, core), device(x, y, z - 4, core)
    z_ahead = device(x, y, z + 8, core)

    def at_y(step, side):
        return (lax.rem(y + step, 4) * 2 + side) * 2 + core

    z_base = z - z_quarter
    z_peers = [device(x, y, z_base + lax.rem(z_quarter + d, 4), core) for d in (1, 2, 3)]
    x_peers = [device(x + d, y, z, core) for d in (1, 2, 3)]

    sent, due = [], {}

    def start(key, copy, gives=None, takes=None):
        sent.append((copy, gives))
        due[key] = (copy, takes)
        if gives is None:
            copy.start()
        else:
            pl.when(gives)(copy.start)

    def arrive(key):
        copy, takes = due.pop(key)
        if takes is None:
            copy.wait_recv()
        else:
            pl.when(takes)(copy.wait_recv)

    def finish():
        for key in list(due):
            arrive(key)
        for copy, gives in sent:
            if gives is None:
                copy.wait_send()
            else:
                pl.when(gives)(copy.wait_send)
        for load in list(loading):
            loaded(load)

    loading = {}

    def load(key, source, target, sem):
        loading[key] = pltpu.make_async_copy(source, target, sem)
        loading[key].start()

    def loaded(key):
        loading.pop(key).wait()

    halves = [pl.ds(n * (CHANNELS // 2), CHANNELS // 2) for n in range(2)]
    for n in range(2):
        load(
            ("x", n), x_hbm.at[:, halves[n]], x_buf.at[pl.ds(0, PIXELS), halves[n]], load_sem.at[n]
        )
        load(
            ("w", n),
            dilated_hbm.at[:, halves[n]],
            w_buf.at[pl.ds(0, TERMS - OWN), halves[n]],
            load_sem.at[2 + n],
        )
        load(
            ("p", n),
            point_hbm.at[:, halves[n]],
            w_buf.at[pl.ds(TERMS - OWN, OWN), halves[n]],
            load_sem.at[4 + n],
        )
    barrier = pltpu.get_barrier_semaphore()
    fixed_peers = (
        [partner, z_up, z_down] + z_peers + x_peers
        + [device(x, y + d, z, c) for d in y_steps for c in range(2)]
    )
    for peer in fixed_peers:
        pl.semaphore_signal(barrier, inc=1, device_id=peer, device_id_type=MESH)
    heard = jnp.int32(len(fixed_peers))
    for slot in range(6):
        @pl.when(sends(slot))
        def _():
            pl.semaphore_signal(
                barrier, inc=1, device_id=(row + row_offset(slot), member), device_id_type=MESH
            )
        heard = heard + sends(slot).astype(jnp.int32)

    load("bias", bias_hbm, bias_ref, load_sem.at[6])
    load("cot", cot_hbm, cot_buf.at[pl.ds(0, PIXELS)], load_sem.at[7])
    for k in range(4):
        load(("project", k), project_hbm.at[k], project.at[:, k], load_sem.at[8 + k])
    load("project_bias", project_bias_hbm, project_bias_ref, load_sem.at[12])
    x_buf[pl.ds(PIXELS, LANES - PIXELS), :] = jnp.zeros((LANES - PIXELS, CHANNELS), BF16)
    cot_buf[pl.ds(PIXELS, LANES - PIXELS), :] = jnp.zeros((LANES - PIXELS, OUTPUTS), BF16)
    for n in range(2):
        for key in ("x", "w", "p"):
            loaded((key, n))
        product = lax.dot_general(
            w_buf[:, halves[n]],
            x_buf[:, halves[n]],
            (((1,), (1,)), ((), ())),
            preferred_element_type=F32,
        )
        taps[...] = product if n == 0 else taps[...] + product
    for block in range(4):
        lanes = pl.multiple_of(block * 512 + half * 256, 256)
        load(
            ("fill", block),
            w_buf.at[:, pl.ds(lanes, 256)],
            w_both.at[pl.ds(0, TERMS), pl.ds(block * 256, 256)],
            fill_sem.at[block],
        )
    column = lax.rem(lax.broadcasted_iota(jnp.int32, (1, LANES), 1), BREADTH)

    def shift_columns(field, amount):
        if amount == 0:
            return field
        inside = jnp.logical_and(column + amount >= 0, column + amount < BREADTH)
        return jnp.where(inside, pltpu.roll(field, (-amount) % LANES, 1), 0.0)

    def tap(k, i, j):
        return taps[pl.ds((9 * k + 3 * i + j) * OWN, OWN), :]

    def row_sum(k, i):
        d = DILATIONS[k]
        return (
            shift_columns(tap(k, i, 0), -d) + tap(k, i, 1) + shift_columns(tap(k, i, 2), d)
        )

    for k in range(3):
        row_send[2 * k] = row_sum(k, 0)
        row_send[2 * k + 1] = row_sum(k, 2)
    pl.semaphore_wait(barrier, heard)
    for n, peer in ((0, z_up), (1, z_down)):
        pl.semaphore_signal(near.at[n], inc=1, device_id=peer, device_id_type=MESH)
    for slot in (4, 5, 2, 3, 0, 1):
        start(
            ("row", slot),
            remote(
                row_send.at[slot], row_recv.at[slot], row_ss.at[slot], row_rs.at[slot],
                (row + row_offset(slot), member),
            ),
            sends(slot),
            gets(slot),
        )

    z_rows = pl.multiple_of(z_quarter * PIECE_ROWS, 16)
    far_rows = pl.multiple_of(TERMS + z_quarter * PIECE_ROWS, 16)
    far_lanes = pl.multiple_of(x * PIECE_LANES, 128)
    give_lanes = pl.multiple_of(x * 512 + (1 - half) * 256, 256)
    for n in range(2):
        pl.semaphore_wait(near.at[n], 1)
    pl.semaphore_signal(far.at[0], inc=1, device_id=z_ahead, device_id_type=MESH)
    start(
        "first",
        remote(
            w_buf.at[pl.ds(z_rows, PIECE_ROWS), pl.ds(give_lanes, PIECE_LANES)],
            w_both.at[pl.ds(far_rows, PIECE_ROWS), pl.ds(far_lanes, PIECE_LANES)],
            first_ss.at[0], first_rs.at[0], eighth,
        ),
    )

    def diagonal(values, size):
        same = lax.broadcasted_iota(jnp.int32, (size, size), 0) == lax.broadcasted_iota(
            jnp.int32, (size, size), 1
        )
        return jnp.sum(
            jnp.where(same, jnp.broadcast_to(values, (size, size)), 0.0), axis=1, keepdims=True
        )

    loaded("bias")
    bias = bias_ref[...]
    biases = [diagonal(bias[k:k + 1, :], OWN) for k in range(4)]
    acts[member, pl.ds(0, OWN), :] = jnp.maximum(
        taps[pl.ds(TERMS - OWN, OWN), :] + biases[0], 0.0
    ).astype(BF16)
    centres = [row_sum(k, 1) + biases[k + 1] for k in range(3)]

    def send_acts(block, part, where, arriving):
        n = len(passed)
        passed.append(block)
        rows = pl.ds(0, 4 * OWN) if part is None else pl.ds(part * 2 * OWN, 2 * OWN)
        place = 0 if part is None else part

        def copy(of):
            ref = acts.at[of, rows]
            return remote(ref, ref, act_ss.at[n], act_rs.at[of, place], where)

        start(("act", n), copy(block))
        due[("act", n)] = (copy(arriving), None)
        return ("act", n)

    passed = []
    from_opposite = []
    for k in range(3):
        total = centres[k]
        for slot in (2 * k, 2 * k + 1):
            arrive(("row", slot))
            total = total + jnp.where(gets(slot), row_recv[slot], 0.0)
        acts[member, pl.ds((k + 1) * OWN, OWN), :] = jnp.maximum(total, 0.0).astype(BF16)
        if k == 0:
            pl.semaphore_wait(far.at[0], 1)
        if k in (0, 2):
            from_opposite.append(send_acts(member, k // 2, opposite, other))
    own_y = {}
    for d in y_steps:
        own_y[4 - d] = send_acts(
            member, None, device(x, y + d, z, core), at_y(4 - d, half)
        )
    rest = [send_acts(member, None, partner, member + twin)]

    for k in range(4):
        loaded(("project", k))
    loaded("cot")
    loaded("project_bias")
    project_t[...] = project[...].reshape(MEMBERS * 4 * OWN, OUTPUTS).T
    cot_t[...] = cot_buf[...].astype(F32).T
    columns[...] = jnp.broadcast_to(diagonal(project_bias_ref[...], OUTPUTS), (OUTPUTS, BLOCK))
    for d in (1, 3, 2):
        arrive(own_y[d])
        block = at_y(d, half)
        rest.append(send_acts(block, None, partner, block + twin))
    def far_piece(d):
        rows_from = pl.multiple_of(
            TERMS + lax.rem(z_quarter + 4 - d, 4) * PIECE_ROWS, 16
        )
        return w_both.at[pl.ds(rows_from, PIECE_ROWS), pl.ds(far_lanes, PIECE_LANES)]

    def spread_x(d):
        for e in (1, 2, 3):
            n = 3 * d + e - 1
            start(
                ("x", d, e),
                remote(far_piece(d), far_piece(d), xg_ss.at[n], xg_rs.at[n], x_peers[e - 1]),
            )

    arrive("first")
    for d in (1, 2, 3):
        start(
            ("z", d),
            remote(
                far_piece(0), far_piece(0), zg_ss.at[d - 1], zg_rs.at[d - 1], z_peers[d - 1]
            ),
        )
    spread_x(0)
    for part in range(2):
        arrive(from_opposite[part])
        for d in y_steps:
            for c in range(2):
                where = device(x, y + d, z, core + c * twin)
                rest.append(send_acts(other, part, where, at_y(4 - d, 1 - half) + c * twin))
        rest.append(send_acts(other, part, partner, other + twin))
        if part == 0:
            for d in (1, 2, 3):
                arrive(("z", d))
                spread_x(d)
    for key in rest:
        arrive(key)
    pre[...] = (
        jnp.dot(
            project_t[...],
            acts[...].reshape(MEMBERS * 4 * OWN, LANES),
            preferred_element_type=F32,
        )
        + columns[:, 0:1]
    )
    head_grad = jnp.where(pre[...] > 0, cot_t[...], 0.0).astype(BF16)
    for side, block in ((0, member), (1, other)):
        act_grad = jnp.dot(
            project[block].reshape(4 * OWN, OUTPUTS), head_grad, preferred_element_type=F32
        )
        branch_grad = jnp.where(acts[block] > 0, act_grad, 0.0).astype(BF16)
        for k in range(4):
            grads[k, pl.ds(side * OWN, OWN), :] = branch_grad[k * OWN:(k + 1) * OWN]
    for slot in (4, 5, 2, 3, 0, 1):
        start(
            ("grad", slot),
            remote(
                grads.at[slot // 2 + 1], grad_recv.at[slot], grow_ss.at[slot], grow_rs.at[slot],
                (row + row_offset(slot), member),
            ),
            sends(slot),
            gets(slot),
        )

    own_head = jnp.maximum(pre[pl.ds(pl.multiple_of(member * OWN, OWN), OWN), :], 0.0)
    for r in range(HEIGHT):
        head_ref[r] = own_head[:, r * BREADTH:(r + 1) * BREADTH].astype(BF16)

    def put(values, t):
        low = values.astype(BF16)
        for side in range(2):
            spread[pl.ds(side * TERMS + t * OWN, OWN), :] = low[side * OWN:(side + 1) * OWN]

    def put_columns(field, k, i):
        for j in range(3):
            put(shift_columns(field, -(j - 1) * DILATIONS[k]), 9 * k + 3 * i + j)

    put(grads[0].astype(F32), TAPS - 1)
    for k in range(3):
        put_columns(grads[k + 1].astype(F32), k, 1)
    for k in range(3):
        for slot, i in ((2 * k, 2), (2 * k + 1, 0)):
            arrive(("grad", slot))
            put_columns(jnp.where(gets(slot), grad_recv[slot].astype(F32), 0.0), k, i)
    spread_t[...] = spread[...].T

    for block in range(4):
        loaded(("fill", block))
    for d in range(4):
        for e in (1, 2, 3):
            arrive(("x", d, e))
    order = (2, 1, 3, 0)

    def multiply(n):
        lanes = pl.multiple_of(lax.rem(y + order[n], 4) * 256, 256)
        product = jnp.dot(
            spread_t[pl.ds(0, PIXELS), :], w_both[:, pl.ds(lanes, 256)], preferred_element_type=F32
        )
        for c in range(2):
            piece = product[:, c * BLOCK:(c + 1) * BLOCK]
            part_sum[n, c] = piece
            part_low[n, c] = piece.astype(BF16)
        start(
            ("core", n),
            remote(part_low.at[n, 1 - core], core_recv.at[n], core_ss.at[n], core_rs.at[n], partner),
        )

    def send_sum(n):
        arrive(("core", n))
        sum_send[n] = (part_sum[n, core] + core_recv[n].astype(F32)).astype(BF16)
        start(
            ("sum", n),
            remote(
                sum_send.at[n], sum_recv.at[n], sum_ss.at[n], sum_rs.at[n],
                device(x, y + order[n], z, core),
            ),
        )

    for n in range(3):
        multiply(n)
    send_sum(0)
    multiply(3)
    send_sum(1)
    send_sum(2)
    arrive(("core", 3))
    total = part_sum[3, core] + core_recv[3].astype(F32)
    for n in (1, 2, 0):
        arrive(("sum", n))
        total = total + sum_recv[n].astype(F32)
    grad_ref[...] = total.astype(BF16)
    finish()


def hand_out(head_in, grad_in, head_out, grad_out, sems):
    copies = [
        pltpu.make_async_copy(head_in, head_out, sems.at[0]),
        pltpu.make_async_copy(grad_in, grad_out, sems.at[1]),
    ]
    for copy in copies:
        copy.start()
    for copy in copies:
        copy.wait()


def on_device(
    features, point_weight, dilated_weight, branch_bias, project_weight, project_bias, cotangent
):
    in_place = pl.BlockSpec(memory_space=pltpu.HBM)
    vmem = pl.BlockSpec(memory_space=pltpu.VMEM)
    dma = pltpu.SemaphoreType.DMA
    head, grad = pl.pallas_call(
        kernel,
        out_shape=(
            jax.ShapeDtypeStruct((HEIGHT, OWN, BREADTH), BF16),
            jax.ShapeDtypeStruct((PIXELS, BLOCK), BF16),
        ),
        in_specs=[in_place] * 7,
        out_specs=(vmem, vmem),
        scratch_shapes=[
            pltpu.VMEM((4, OWN), F32),
            pltpu.VMEM((1, OUTPUTS), F32),
            pltpu.VMEM((LANES, CHANNELS), BF16),
            pltpu.VMEM((TERMS, CHANNELS), BF16),
            pltpu.VMEM((2 * TERMS, CHANNELS // 2), BF16),
            pltpu.VMEM((MEMBERS, 4, OWN, OUTPUTS), BF16),
            pltpu.VMEM((OUTPUTS, MEMBERS * 4 * OWN), BF16),
            pltpu.VMEM((LANES, OUTPUTS), BF16),
            pltpu.VMEM((OUTPUTS, LANES), F32),
            pltpu.VMEM((OUTPUTS, BLOCK), F32),
            pltpu.VMEM((TERMS, LANES), F32),
            pltpu.VMEM((6, OWN, LANES), F32),
            pltpu.VMEM((6, OWN, LANES), F32),
            pltpu.VMEM((MEMBERS, 4 * OWN, LANES), BF16),
            pltpu.VMEM((OUTPUTS, LANES), F32),
            pltpu.VMEM((4, 2 * OWN, LANES), BF16),
            pltpu.VMEM((6, 2 * OWN, LANES), BF16),
            pltpu.VMEM((2 * TERMS, LANES), BF16),
            pltpu.VMEM((LANES, 2 * TERMS), BF16),
            pltpu.VMEM((4, 2, PIXELS, BLOCK), F32),
            pltpu.VMEM((4, 2, PIXELS, BLOCK), BF16),
            pltpu.VMEM((4, PIXELS, BLOCK), BF16),
            pltpu.VMEM((3, PIXELS, BLOCK), BF16),
            pltpu.VMEM((3, PIXELS, BLOCK), BF16),
            pltpu.SemaphoreType.REGULAR((2,)), pltpu.SemaphoreType.REGULAR((1,)),
            dma((13,)), dma((4,)), dma((6,)), dma((6,)), dma((23,)), dma((16, 2)),
            dma((1,)), dma((1,)), dma((3,)), dma((3,)), dma((12,)), dma((12,)),
            dma((6,)), dma((6,)), dma((4,)), dma((4,)), dma((3,)), dma((3,)),
        ],
        compiler_params=pltpu.CompilerParams(
            collective_id=0, has_side_effects=True, vmem_limit_bytes=58 * 1024 * 1024
        ),
        name="pyramid",
    )(
        features.reshape(PIXELS, CHANNELS),
        jnp.transpose(dilated_weight, (0, 1, 2, 4, 3)).reshape(TERMS - OWN, CHANNELS),
        point_weight.T,
        project_weight.reshape(4, MEMBERS, OWN, OUTPUTS),
        cotangent.reshape(PIXELS, OUTPUTS),
        branch_bias,
        project_bias.reshape(1, OUTPUTS),
    )
    head, grad = pl.pallas_call(
        hand_out,
        out_shape=(
            jax.ShapeDtypeStruct((HEIGHT, OWN, BREADTH), BF16),
            jax.ShapeDtypeStruct((PIXELS, BLOCK), BF16),
        ),
        in_specs=[vmem] * 2,
        out_specs=(in_place, in_place),
        scratch_shapes=[dma((2,))],
        name="hand_out",
    )(head, grad)
    return (jnp.transpose(head, (0, 2, 1)), grad.reshape(HEIGHT, BREADTH, BLOCK))


def solution(mesh):
    in_specs = (
        P("rows", None, None),
        P(None, "filt"),
        P(None, None, None, None, "filt"),
        P(None, "filt"),
        P(),
        P(),
        P("rows", None, None),
    )
    out_specs = (P("rows", None, "filt"), P("rows", None, "filt"))
    return jax.shard_map(
        on_device, mesh=mesh, in_specs=in_specs, out_specs=out_specs, check_vma=False
    )
```

```python
import jax
import jax.numpy as jnp
from jax import lax
from jax.experimental import pallas as pl
from jax.experimental.pallas import tpu as pltpu
from jax.sharding import PartitionSpec as P

FIRST_DILATION = 12
SECOND_DILATION = 24
THIRD_DILATION = 36
DILATIONS = (FIRST_DILATION, SECOND_DILATION, THIRD_DILATION)
ROW_BLOCKS = 64
HEIGHT = 12
BREADTH = 48
PIXELS = HEIGHT * BREADTH
LANES = 640
CHANNELS = 2048
OWN = 16
TAPS = 28
TERMS = TAPS * OWN
MEMBERS = 16
OUTPUTS = 256
BLOCK = 128
PIECE_ROWS = TERMS // 4
PIECE_LANES = 256
MESH = pl.DeviceIdType.MESH
BF16 = jnp.bfloat16
F32 = jnp.float32


def device(x, y, z, core):
    x, y, z = lax.rem(x + 4, 4), lax.rem(y + 4, 4), lax.rem(z + 32, 32)
    return (lax.rem(z, 16) * 4 + x, (y * 2 + z // 16) * 2 + core)


def remote(source, target, send_sem, recv_sem, where):
    return pltpu.make_async_remote_copy(
        src_ref=source,
        dst_ref=target,
        send_sem=send_sem,
        recv_sem=recv_sem,
        device_id=where,
        device_id_type=MESH,
    )


def kernel(
    x_hbm, dilated_hbm, point_hbm, project_hbm, cot_hbm, bias_hbm, project_bias_hbm,
    head_ref, grad_ref,
    bias_ref, project_bias_ref, x_buf, w_buf, w_both, project, project_t, cot_buf, cot_t, columns,
    taps, row_send, row_recv, acts, pre, grads, grad_recv, spread, spread_t,
    part_sum, part_low, core_recv, sum_send, sum_recv,
    far, load_sem, fill_sem, row_ss, row_rs, act_ss, act_rs, first_ss, first_rs, zg_ss, zg_rs,
    xg_ss, xg_rs, grow_ss, grow_rs, core_ss, core_rs, sum_ss, sum_rs,
):
    row = lax.axis_index("rows")
    member = lax.axis_index("filt")
    x, z_low = lax.rem(row, 4), row // 4
    y, half, core = member // 4, lax.rem(member // 2, 2), lax.rem(member, 2)
    z = half * 16 + z_low
    z_quarter = lax.rem(z_low, 4)
    other = member + 2 - 4 * half
    twin = 1 - 2 * core

    def row_offset(slot):
        return (slot // 2 + 1) * (1 - 2 * (slot % 2))

    def sends(slot):
        place = row + row_offset(slot)
        return jnp.logical_and(place >= 0, place < ROW_BLOCKS)

    def gets(slot):
        place = row - row_offset(slot)
        return jnp.logical_and(place >= 0, place < ROW_BLOCKS)

    opposite = device(x, y, z + 16, core)
    eighth = device(x, y, z + jnp.where(z_low >= 8, 8, -8), core)
    partner = device(x, y, z, 1 - core)
    y_steps = (2, 1, 3)
    z_ahead, z_behind = device(x, y, z + 8, core), device(x, y, z - 8, core)

    def at_y(step, side):
        return (lax.rem(y + step, 4) * 2 + side) * 2 + core

    z_base = z - z_quarter
    z_peers = [device(x, y, z_base + lax.rem(z_quarter + d, 4), core) for d in (1, 2, 3)]
    x_peers = [device(x + d, y, z, core) for d in (1, 2, 3)]

    sent, due = [], {}

    def start(key, copy, gives=None, takes=None):
        sent.append((copy, gives))
        due[key] = (copy, takes)
        if gives is None:
            copy.start()
        else:
            pl.when(gives)(copy.start)

    def arrive(key):
        copy, takes = due.pop(key)
        if takes is None:
            copy.wait_recv()
        else:
            pl.when(takes)(copy.wait_recv)

    def drain():
        for copy, gives in sent:
            if gives is None:
                copy.wait_send()
            else:
                pl.when(gives)(copy.wait_send)
        sent.clear()

    def finish():
        for key in list(due):
            arrive(key)
        drain()
        for load in list(loading):
            loaded(load)

    loading = {}

    def load(key, source, target, sem):
        loading[key] = pltpu.make_async_copy(source, target, sem)
        loading[key].start()

    def loaded(key):
        loading.pop(key).wait()

    halves = [pl.ds(n * (CHANNELS // 2), CHANNELS // 2) for n in range(2)]
    for n in range(2):
        load(
            ("x", n), x_hbm.at[:, halves[n]], x_buf.at[pl.ds(0, PIXELS), halves[n]], load_sem.at[n]
        )
        load(
            ("w", n),
            dilated_hbm.at[:, halves[n]],
            w_buf.at[pl.ds(0, TERMS - OWN), halves[n]],
            load_sem.at[2 + n],
        )
        load(
            ("p", n),
            point_hbm.at[:, halves[n]],
            w_buf.at[pl.ds(TERMS - OWN, OWN), halves[n]],
            load_sem.at[4 + n],
        )
    barrier = pltpu.get_barrier_semaphore()
    fixed_peers = (
        [partner, z_ahead, z_behind] + z_peers + x_peers
        + [device(x, y + d, z, c) for d in y_steps for c in range(2)]
    )
    for peer in fixed_peers:
        pl.semaphore_signal(barrier, inc=1, device_id=peer, device_id_type=MESH)
    heard = jnp.int32(len(fixed_peers))
    for slot in range(6):
        @pl.when(sends(slot))
        def _():
            pl.semaphore_signal(
                barrier, inc=1, device_id=(row + row_offset(slot), member), device_id_type=MESH
            )
        heard = heard + sends(slot).astype(jnp.int32)

    load("bias", bias_hbm, bias_ref, load_sem.at[6])
    load("cot", cot_hbm, cot_buf.at[pl.ds(0, PIXELS)], load_sem.at[7])
    for k in range(4):
        load(("project", k), project_hbm.at[k], project.at[:, k], load_sem.at[8 + k])
    load("project_bias", project_bias_hbm, project_bias_ref, load_sem.at[12])
    x_buf[pl.ds(PIXELS, LANES - PIXELS), :] = jnp.zeros((LANES - PIXELS, CHANNELS), BF16)
    cot_buf[pl.ds(PIXELS, LANES - PIXELS), :] = jnp.zeros((LANES - PIXELS, OUTPUTS), BF16)
    for n in range(2):
        for key in ("x", "w", "p"):
            loaded((key, n))
        product = lax.dot_general(
            w_buf[:, halves[n]],
            x_buf[:, halves[n]],
            (((1,), (1,)), ((), ())),
            preferred_element_type=F32,
        )
        taps[...] = product if n == 0 else taps[...] + product
    order = (2, 1, 3, 0)
    for n in range(4):
        lanes = pl.multiple_of(lax.rem(y + order[n], 4) * 512 + half * 256, 256)
        load(
            ("fill", n),
            w_buf.at[:, pl.ds(lanes, 256)],
            w_both.at[pl.ds(0, TERMS), pl.ds(n * 256, 256)],
            fill_sem.at[n],
        )
    column = lax.rem(lax.broadcasted_iota(jnp.int32, (1, LANES), 1), BREADTH)

    def shift_columns(field, amount):
        if amount == 0:
            return field
        inside = jnp.logical_and(column + amount >= 0, column + amount < BREADTH)
        return jnp.where(inside, pltpu.roll(field, (-amount) % LANES, 1), 0.0)

    def tap(k, i, j):
        return taps[pl.ds((9 * k + 3 * i + j) * OWN, OWN), :]

    def row_sum(k, i):
        d = DILATIONS[k]
        return (
            shift_columns(tap(k, i, 0), -d) + tap(k, i, 1) + shift_columns(tap(k, i, 2), d)
        )

    for k in range(3):
        row_send[2 * k] = row_sum(k, 0)
        row_send[2 * k + 1] = row_sum(k, 2)
    pl.semaphore_wait(barrier, heard)
    pl.semaphore_signal(far.at[0], inc=1, device_id=z_ahead, device_id_type=MESH)
    for slot in (4, 5, 2, 3, 0, 1):
        start(
            ("row", slot),
            remote(
                row_send.at[slot], row_recv.at[slot], row_ss.at[slot], row_rs.at[slot],
                (row + row_offset(slot), member),
            ),
            sends(slot),
            gets(slot),
        )

    z_rows = pl.multiple_of(z_quarter * PIECE_ROWS, 16)
    far_rows = pl.multiple_of(TERMS + z_quarter * PIECE_ROWS, 16)
    far_lanes = pl.multiple_of(x * PIECE_LANES, 128)
    ahead = jnp.where(x == 0, 2, jnp.where(x == 1, 1, jnp.where(x == 2, 3, 0)))
    give_lanes = pl.multiple_of(lax.rem(y + ahead, 4) * 512 + (1 - half) * 256, 256)
    start(
        "first",
        remote(
            w_buf.at[pl.ds(z_rows, PIECE_ROWS), pl.ds(give_lanes, PIECE_LANES)],
            w_both.at[pl.ds(far_rows, PIECE_ROWS), pl.ds(far_lanes, PIECE_LANES)],
            first_ss.at[0], first_rs.at[0], eighth,
        ),
    )

    def diagonal(values, size):
        same = lax.broadcasted_iota(jnp.int32, (size, size), 0) == lax.broadcasted_iota(
            jnp.int32, (size, size), 1
        )
        return jnp.sum(
            jnp.where(same, jnp.broadcast_to(values, (size, size)), 0.0), axis=1, keepdims=True
        )

    loaded("bias")
    bias = bias_ref[...]
    biases = [diagonal(bias[k:k + 1, :], OWN) for k in range(4)]
    acts[member, pl.ds(0, OWN), :] = jnp.maximum(
        taps[pl.ds(TERMS - OWN, OWN), :] + biases[0], 0.0
    ).astype(BF16)
    centres = [row_sum(k, 1) + biases[k + 1] for k in range(3)]

    def send_acts(block, part, where, arriving):
        n = len(passed)
        passed.append(block)
        rows = pl.ds(0, 4 * OWN) if part is None else pl.ds(part * OWN, OWN)
        place = 0 if part is None else part

        def copy(of):
            ref = acts.at[of, rows]
            return remote(ref, ref, act_ss.at[n], act_rs.at[of, place], where)

        start(("act", n), copy(block))
        due[("act", n)] = (copy(arriving), None)
        return ("act", n)

    passed = []
    from_opposite = []
    for k in range(3):
        total = centres[k]
        for slot in (2 * k, 2 * k + 1):
            arrive(("row", slot))
            total = total + jnp.where(gets(slot), row_recv[slot], 0.0)
        acts[member, pl.ds((k + 1) * OWN, OWN), :] = jnp.maximum(total, 0.0).astype(BF16)
        if k == 0:
            pl.semaphore_wait(far.at[0], 1)
            from_opposite.append(send_acts(member, 0, opposite, other))
        from_opposite.append(send_acts(member, k + 1, opposite, other))
    own_y = {}
    for d in y_steps:
        own_y[4 - d] = send_acts(
            member, None, device(x, y + d, z, core), at_y(4 - d, half)
        )
    rest = [send_acts(member, None, partner, member + twin)]

    for k in range(4):
        loaded(("project", k))
    loaded("cot")
    loaded("project_bias")
    project_t[...] = project[...].reshape(MEMBERS * 4 * OWN, OUTPUTS).T
    cot_t[...] = cot_buf[...].astype(F32).T
    columns[...] = jnp.broadcast_to(diagonal(project_bias_ref[...], OUTPUTS), (OUTPUTS, BLOCK))
    for d in (1, 3, 2):
        arrive(own_y[d])
        block = at_y(d, half)
        rest.append(send_acts(block, None, partner, block + twin))
    def far_piece(d):
        rows_from = pl.multiple_of(
            TERMS + lax.rem(z_quarter + 4 - d, 4) * PIECE_ROWS, 16
        )
        return w_both.at[pl.ds(rows_from, PIECE_ROWS), pl.ds(far_lanes, PIECE_LANES)]

    def spread_x(d):
        for e in (1, 2, 3):
            n = 3 * d + e - 1
            start(
                ("x", d, e),
                remote(far_piece(d), far_piece(d), xg_ss.at[n], xg_rs.at[n], x_peers[e - 1]),
            )

    arrive("first")
    for d in (1, 2, 3):
        start(
            ("z", d),
            remote(
                far_piece(0), far_piece(0), zg_ss.at[d - 1], zg_rs.at[d - 1], z_peers[d - 1]
            ),
        )
    spread_x(0)
    for part in range(4):
        arrive(from_opposite[part])
        for d in y_steps:
            for c in range(2):
                where = device(x, y + d, z, core + c * twin)
                rest.append(send_acts(other, part, where, at_y(4 - d, 1 - half) + c * twin))
        rest.append(send_acts(other, part, partner, other + twin))
        if part == 0:
            for d in (1, 2, 3):
                arrive(("z", d))
                spread_x(d)
    for key in rest:
        arrive(key)
    pre[...] = (
        jnp.dot(
            project_t[...],
            acts[...].reshape(MEMBERS * 4 * OWN, LANES),
            preferred_element_type=F32,
        )
        + columns[:, 0:1]
    )
    head_grad = jnp.where(pre[...] > 0, cot_t[...], 0.0).astype(BF16)
    branch_grads = []
    for block in (member, other):
        act_grad = jnp.dot(
            project[block].reshape(4 * OWN, OUTPUTS), head_grad, preferred_element_type=F32
        )
        branch_grads.append(jnp.where(acts[block] > 0, act_grad, 0.0).astype(BF16))
    for k in (3, 2, 1, 0):
        for side in range(2):
            grads[k, pl.ds(side * OWN, OWN), :] = branch_grads[side][k * OWN:(k + 1) * OWN]
        for slot in (2 * k - 2, 2 * k - 1) if k else ():
            start(
                ("grad", slot),
                remote(
                    grads.at[k], grad_recv.at[slot], grow_ss.at[slot], grow_rs.at[slot],
                    (row + row_offset(slot), member),
                ),
                sends(slot),
                gets(slot),
            )
    own_head = jnp.maximum(pre[pl.ds(pl.multiple_of(member * OWN, OWN), OWN), :], 0.0)
    for r in range(HEIGHT):
        head_ref[r] = own_head[:, r * BREADTH:(r + 1) * BREADTH].astype(BF16)

    def put(values, t):
        low = values.astype(BF16)
        for side in range(2):
            spread[pl.ds(side * TERMS + t * OWN, OWN), :] = low[side * OWN:(side + 1) * OWN]

    def put_columns(field, k, i):
        for j in range(3):
            put(shift_columns(field, -(j - 1) * DILATIONS[k]), 9 * k + 3 * i + j)

    put(grads[0].astype(F32), TAPS - 1)
    for k in range(3):
        put_columns(grads[k + 1].astype(F32), k, 1)
    for k in range(3):
        for slot, i in ((2 * k, 2), (2 * k + 1, 0)):
            arrive(("grad", slot))
            put_columns(jnp.where(gets(slot), grad_recv[slot].astype(F32), 0.0), k, i)
    spread_t[...] = spread[...].T

    for block in range(4):
        loaded(("fill", block))
    for d in range(4):
        for e in (1, 2, 3):
            arrive(("x", d, e))
    def multiply(pair):
        product = jnp.dot(
            spread_t[pl.ds(0, PIXELS), :],
            w_both[:, pl.ds(pair * 512, 512)],
            preferred_element_type=F32,
        )
        for n in (2 * pair, 2 * pair + 1):
            for c in range(2):
                lane = (n % 2) * 256 + c * BLOCK
                piece = product[:, lane:lane + BLOCK]
                part_sum[n, c] = piece
                part_low[n, c] = piece.astype(BF16)
            start(
                ("core", n),
                remote(
                    part_low.at[n, 1 - core], core_recv.at[n], core_ss.at[n], core_rs.at[n],
                    partner,
                ),
            )

    def send_sum(n):
        arrive(("core", n))
        sum_send[n] = (part_sum[n, core] + core_recv[n].astype(F32)).astype(BF16)
        start(
            ("sum", n),
            remote(
                sum_send.at[n], sum_recv.at[n], sum_ss.at[n], sum_rs.at[n],
                device(x, y + order[n], z, core),
            ),
        )

    multiply(0)
    multiply(1)
    for n in range(3):
        send_sum(n)
    drain()
    arrive(("core", 3))
    total = part_sum[3, core] + core_recv[3].astype(F32)
    for n in (1, 2, 0):
        arrive(("sum", n))
        total = total + sum_recv[n].astype(F32)
    grad_ref[...] = total.astype(BF16)
    finish()


def hand_out(head_in, grad_in, head_out, grad_out, sems):
    copies = [
        pltpu.make_async_copy(head_in, head_out, sems.at[0]),
        pltpu.make_async_copy(grad_in, grad_out, sems.at[1]),
    ]
    for copy in copies:
        copy.start()
    for copy in copies:
        copy.wait()


def on_device(
    features, point_weight, dilated_weight, branch_bias, project_weight, project_bias, cotangent
):
    in_place = pl.BlockSpec(memory_space=pltpu.HBM)
    vmem = pl.BlockSpec(memory_space=pltpu.VMEM)
    dma = pltpu.SemaphoreType.DMA
    head, grad = pl.pallas_call(
        kernel,
        out_shape=(
            pltpu.VMEM((HEIGHT, OWN, BREADTH), BF16),
            pltpu.VMEM((PIXELS, BLOCK), BF16),
        ),
        in_specs=[in_place] * 7,
        out_specs=(vmem, vmem),
        scratch_shapes=[
            pltpu.VMEM((4, OWN), F32),
            pltpu.VMEM((1, OUTPUTS), F32),
            pltpu.VMEM((LANES, CHANNELS), BF16),
            pltpu.VMEM((TERMS, CHANNELS), BF16),
            pltpu.VMEM((2 * TERMS, CHANNELS // 2), BF16),
            pltpu.VMEM((MEMBERS, 4, OWN, OUTPUTS), BF16),
            pltpu.VMEM((OUTPUTS, MEMBERS * 4 * OWN), BF16),
            pltpu.VMEM((LANES, OUTPUTS), BF16),
            pltpu.VMEM((OUTPUTS, LANES), F32),
            pltpu.VMEM((OUTPUTS, BLOCK), F32),
            pltpu.VMEM((TERMS, LANES), F32),
            pltpu.VMEM((6, OWN, LANES), F32),
            pltpu.VMEM((6, OWN, LANES), F32),
            pltpu.VMEM((MEMBERS, 4 * OWN, LANES), BF16),
            pltpu.VMEM((OUTPUTS, LANES), F32),
            pltpu.VMEM((4, 2 * OWN, LANES), BF16),
            pltpu.VMEM((6, 2 * OWN, LANES), BF16),
            pltpu.VMEM((2 * TERMS, LANES), BF16),
            pltpu.VMEM((LANES, 2 * TERMS), BF16),
            pltpu.VMEM((4, 2, PIXELS, BLOCK), F32),
            pltpu.VMEM((4, 2, PIXELS, BLOCK), BF16),
            pltpu.VMEM((4, PIXELS, BLOCK), BF16),
            pltpu.VMEM((3, PIXELS, BLOCK), BF16),
            pltpu.VMEM((3, PIXELS, BLOCK), BF16),
            pltpu.SemaphoreType.REGULAR((1,)),
            dma((13,)), dma((4,)), dma((6,)), dma((6,)), dma((39,)), dma((16, 4)),
            dma((1,)), dma((1,)), dma((3,)), dma((3,)), dma((12,)), dma((12,)),
            dma((6,)), dma((6,)), dma((4,)), dma((4,)), dma((3,)), dma((3,)),
        ],
        compiler_params=pltpu.CompilerParams(
            collective_id=0, has_side_effects=True, vmem_limit_bytes=58 * 1024 * 1024
        ),
        name="pyramid",
    )(
        features.reshape(PIXELS, CHANNELS),
        jnp.transpose(dilated_weight, (0, 1, 2, 4, 3)).reshape(TERMS - OWN, CHANNELS),
        point_weight.T,
        project_weight.reshape(4, MEMBERS, OWN, OUTPUTS),
        cotangent.reshape(PIXELS, OUTPUTS),
        branch_bias,
        project_bias.reshape(1, OUTPUTS),
    )
    head, grad = pl.pallas_call(
        hand_out,
        out_shape=(
            jax.ShapeDtypeStruct((HEIGHT, OWN, BREADTH), BF16),
            jax.ShapeDtypeStruct((PIXELS, BLOCK), BF16),
        ),
        in_specs=[vmem] * 2,
        out_specs=(in_place, in_place),
        scratch_shapes=[dma((2,))],
        name="hand_out",
    )(*[pltpu.with_memory_space_constraint(value, pltpu.VMEM) for value in (head, grad)])
    return (jnp.transpose(head, (0, 2, 1)), grad.reshape(HEIGHT, BREADTH, BLOCK))


def solution(mesh):
    in_specs = (
        P("rows", None, None),
        P(None, "filt"),
        P(None, None, None, None, "filt"),
        P(None, "filt"),
        P(),
        P(),
        P("rows", None, None),
    )
    out_specs = (P("rows", None, "filt"), P("rows", None, "filt"))
    return jax.shard_map(
        on_device, mesh=mesh, in_specs=in_specs, out_specs=out_specs, check_vma=False
    )
```

```python
import jax
import jax.numpy as jnp
from jax import lax
from jax.experimental import pallas as pl
from jax.experimental.pallas import tpu as pltpu
from jax.sharding import PartitionSpec as P

FIRST_DILATION = 12
SECOND_DILATION = 24
THIRD_DILATION = 36
DILATIONS = (FIRST_DILATION, SECOND_DILATION, THIRD_DILATION)
ROW_BLOCKS = 64
HEIGHT = 12
BREADTH = 48
PIXELS = HEIGHT * BREADTH
LANES = 640
CHANNELS = 2048
OWN = 16
TAPS = 28
TERMS = TAPS * OWN
MEMBERS = 16
OUTPUTS = 256
BLOCK = 128
PIECE_ROWS = TERMS // 4
PIECE_LANES = 256
MESH = pl.DeviceIdType.MESH
BF16 = jnp.bfloat16
F32 = jnp.float32


def device(x, y, z, core):
    x, y, z = lax.rem(x + 4, 4), lax.rem(y + 4, 4), lax.rem(z + 32, 32)
    return (lax.rem(z, 16) * 4 + x, (y * 2 + z // 16) * 2 + core)


def remote(source, target, send_sem, recv_sem, where):
    return pltpu.make_async_remote_copy(
        src_ref=source,
        dst_ref=target,
        send_sem=send_sem,
        recv_sem=recv_sem,
        device_id=where,
        device_id_type=MESH,
    )


def kernel(
    x_hbm, dilated_hbm, point_hbm, project_hbm, cot_hbm, bias_hbm, project_bias_hbm,
    head_ref, grad_ref,
    bias_ref, project_bias_ref, x_buf, w_buf, w_both, project, project_t, cot_buf, cot_t, columns,
    taps, row_send, row_recv, acts, pre, grads, grad_recv, spread, spread_t,
    part_sum, part_low, core_recv, sum_send, sum_recv,
    far, load_sem, fill_sem, row_ss, row_rs, act_ss, act_rs, first_ss, first_rs, zg_ss, zg_rs,
    xg_ss, xg_rs, grow_ss, grow_rs, core_ss, core_rs, sum_ss, sum_rs,
):
    row = lax.axis_index("rows")
    member = lax.axis_index("filt")
    x, z_low = lax.rem(row, 4), row // 4
    y, half, core = member // 4, lax.rem(member // 2, 2), lax.rem(member, 2)
    z = half * 16 + z_low
    z_quarter = lax.rem(z_low, 4)
    other = member + 2 - 4 * half
    twin = 1 - 2 * core

    def row_offset(slot):
        return (slot // 2 + 1) * (1 - 2 * (slot % 2))

    def sends(slot):
        place = row + row_offset(slot)
        return jnp.logical_and(place >= 0, place < ROW_BLOCKS)

    def gets(slot):
        place = row - row_offset(slot)
        return jnp.logical_and(place >= 0, place < ROW_BLOCKS)

    opposite = device(x, y, z + 16, core)
    eighth = device(x, y, z + jnp.where(z_low >= 8, 8, -8), core)
    partner = device(x, y, z, 1 - core)
    y_steps = (2, 1, 3)
    z_ahead, z_behind = device(x, y, z + 8, core), device(x, y, z - 8, core)

    def at_y(step, side):
        return (lax.rem(y + step, 4) * 2 + side) * 2 + core

    z_base = z - z_quarter
    z_peers = [device(x, y, z_base + lax.rem(z_quarter + d, 4), core) for d in (1, 2, 3)]
    x_peers = [device(x + d, y, z, core) for d in (1, 2, 3)]

    sent, due = [], {}

    def start(key, copy, gives=None, takes=None):
        sent.append((copy, gives))
        due[key] = (copy, takes)
        if gives is None:
            copy.start()
        else:
            pl.when(gives)(copy.start)

    def arrive(key):
        copy, takes = due.pop(key)
        if takes is None:
            copy.wait_recv()
        else:
            pl.when(takes)(copy.wait_recv)

    def drain():
        for copy, gives in sent:
            if gives is None:
                copy.wait_send()
            else:
                pl.when(gives)(copy.wait_send)
        sent.clear()

    def finish():
        for key in list(due):
            arrive(key)
        drain()
        for load in list(loading):
            loaded(load)

    loading = {}

    def load(key, source, target, sem):
        loading[key] = pltpu.make_async_copy(source, target, sem)
        loading[key].start()

    def loaded(key):
        loading.pop(key).wait()

    halves = [pl.ds(n * (CHANNELS // 2), CHANNELS // 2) for n in range(2)]
    for n in range(2):
        load(
            ("x", n), x_hbm.at[:, halves[n]], x_buf.at[pl.ds(0, PIXELS), halves[n]], load_sem.at[n]
        )
        load(
            ("w", n),
            dilated_hbm.at[:, halves[n]],
            w_buf.at[pl.ds(0, TERMS - OWN), halves[n]],
            load_sem.at[2 + n],
        )
        load(
            ("p", n),
            point_hbm.at[:, halves[n]],
            w_buf.at[pl.ds(TERMS - OWN, OWN), halves[n]],
            load_sem.at[4 + n],
        )
    barrier = pltpu.get_barrier_semaphore()
    fixed_peers = (
        [partner, z_ahead, z_behind] + z_peers + x_peers
        + [device(x, y + d, z, c) for d in y_steps for c in range(2)]
    )
    for peer in fixed_peers:
        pl.semaphore_signal(barrier, inc=1, device_id=peer, device_id_type=MESH)
    heard = jnp.int32(len(fixed_peers))
    for slot in range(6):
        @pl.when(sends(slot))
        def _():
            pl.semaphore_signal(
                barrier, inc=1, device_id=(row + row_offset(slot), member), device_id_type=MESH
            )
        heard = heard + sends(slot).astype(jnp.int32)

    load("bias", bias_hbm, bias_ref, load_sem.at[6])
    load("cot", cot_hbm, cot_buf.at[pl.ds(0, PIXELS)], load_sem.at[7])
    for k in range(4):
        load(("project", k), project_hbm.at[k], project.at[:, k], load_sem.at[8 + k])
    load("project_bias", project_bias_hbm, project_bias_ref, load_sem.at[12])
    x_buf[pl.ds(PIXELS, LANES - PIXELS), :] = jnp.zeros((LANES - PIXELS, CHANNELS), BF16)
    cot_buf[pl.ds(PIXELS, LANES - PIXELS), :] = jnp.zeros((LANES - PIXELS, OUTPUTS), BF16)
    for n in range(2):
        for key in ("x", "w", "p"):
            loaded((key, n))
        product = lax.dot_general(
            w_buf[:, halves[n]],
            x_buf[:, halves[n]],
            (((1,), (1,)), ((), ())),
            preferred_element_type=F32,
        )
        taps[...] = product if n == 0 else taps[...] + product
    order = (2, 1, 3, 0)
    for n in range(4):
        lanes = pl.multiple_of(lax.rem(y + order[n], 4) * 512 + half * 256, 256)
        load(
            ("fill", n),
            w_buf.at[:, pl.ds(lanes, 256)],
            w_both.at[pl.ds(0, TERMS), pl.ds(n * 256, 256)],
            fill_sem.at[n],
        )
    column = lax.rem(lax.broadcasted_iota(jnp.int32, (1, LANES), 1), BREADTH)

    def shift_columns(field, amount):
        if amount == 0:
            return field
        inside = jnp.logical_and(column + amount >= 0, column + amount < BREADTH)
        return jnp.where(inside, pltpu.roll(field, (-amount) % LANES, 1), 0.0)

    def tap(k, i, j):
        return taps[pl.ds((9 * k + 3 * i + j) * OWN, OWN), :]

    def row_sum(k, i):
        d = DILATIONS[k]
        return (
            shift_columns(tap(k, i, 0), -d) + tap(k, i, 1) + shift_columns(tap(k, i, 2), d)
        )

    for k in range(3):
        row_send[2 * k] = row_sum(k, 0)
        row_send[2 * k + 1] = row_sum(k, 2)
    pl.semaphore_wait(barrier, heard)
    pl.semaphore_signal(far.at[0], inc=1, device_id=z_ahead, device_id_type=MESH)
    for slot in (4, 5, 2, 3, 0, 1):
        start(
            ("row", slot),
            remote(
                row_send.at[slot], row_recv.at[slot], row_ss.at[slot], row_rs.at[slot],
                (row + row_offset(slot), member),
            ),
            sends(slot),
            gets(slot),
        )

    z_rows = pl.multiple_of(z_quarter * PIECE_ROWS, 16)
    far_rows = pl.multiple_of(TERMS + z_quarter * PIECE_ROWS, 16)
    far_lanes = pl.multiple_of(x * PIECE_LANES, 128)
    ahead = jnp.where(x == 0, 2, jnp.where(x == 1, 1, jnp.where(x == 2, 3, 0)))
    give_lanes = pl.multiple_of(lax.rem(y + ahead, 4) * 512 + (1 - half) * 256, 256)
    start(
        "first",
        remote(
            w_buf.at[pl.ds(z_rows, PIECE_ROWS), pl.ds(give_lanes, PIECE_LANES)],
            w_both.at[pl.ds(far_rows, PIECE_ROWS), pl.ds(far_lanes, PIECE_LANES)],
            first_ss.at[0], first_rs.at[0], eighth,
        ),
    )

    def diagonal(values, size):
        same = lax.broadcasted_iota(jnp.int32, (size, size), 0) == lax.broadcasted_iota(
            jnp.int32, (size, size), 1
        )
        return jnp.sum(
            jnp.where(same, jnp.broadcast_to(values, (size, size)), 0.0), axis=1, keepdims=True
        )

    loaded("bias")
    bias = bias_ref[...]
    biases = [diagonal(bias[k:k + 1, :], OWN) for k in range(4)]
    acts[member, pl.ds(0, OWN), :] = jnp.maximum(
        taps[pl.ds(TERMS - OWN, OWN), :] + biases[0], 0.0
    ).astype(BF16)
    centres = [row_sum(k, 1) + biases[k + 1] for k in range(3)]

    def send_acts(block, part, where, arriving):
        n = len(passed)
        passed.append(block)
        rows = pl.ds(0, 4 * OWN) if part is None else pl.ds(part * 2 * OWN, 2 * OWN)
        place = 0 if part is None else part

        def copy(of):
            ref = acts.at[of, rows]
            return remote(ref, ref, act_ss.at[n], act_rs.at[of, place], where)

        start(("act", n), copy(block))
        due[("act", n)] = (copy(arriving), None)
        return ("act", n)

    passed = []
    from_opposite = []
    for k in range(3):
        total = centres[k]
        for slot in (2 * k, 2 * k + 1):
            arrive(("row", slot))
            total = total + jnp.where(gets(slot), row_recv[slot], 0.0)
        acts[member, pl.ds((k + 1) * OWN, OWN), :] = jnp.maximum(total, 0.0).astype(BF16)
        if k == 0:
            pl.semaphore_wait(far.at[0], 1)
        if k in (0, 2):
            from_opposite.append(send_acts(member, k // 2, opposite, other))
    own_y = {}
    for d in y_steps:
        own_y[4 - d] = send_acts(
            member, None, device(x, y + d, z, core), at_y(4 - d, half)
        )
    rest = [send_acts(member, None, partner, member + twin)]

    for k in range(4):
        loaded(("project", k))
    loaded("cot")
    loaded("project_bias")
    project_t[...] = project[...].reshape(MEMBERS * 4 * OWN, OUTPUTS).T
    cot_t[...] = cot_buf[...].astype(F32).T
    columns[...] = jnp.broadcast_to(diagonal(project_bias_ref[...], OUTPUTS), (OUTPUTS, BLOCK))
    for d in (1, 3, 2):
        arrive(own_y[d])
        block = at_y(d, half)
        rest.append(send_acts(block, None, partner, block + twin))
    def far_piece(d):
        rows_from = pl.multiple_of(
            TERMS + lax.rem(z_quarter + 4 - d, 4) * PIECE_ROWS, 16
        )
        return w_both.at[pl.ds(rows_from, PIECE_ROWS), pl.ds(far_lanes, PIECE_LANES)]

    def spread_x(d):
        for e in (1, 2, 3):
            n = 3 * d + e - 1
            start(
                ("x", d, e),
                remote(far_piece(d), far_piece(d), xg_ss.at[n], xg_rs.at[n], x_peers[e - 1]),
            )

    arrive("first")
    spread_x(0)
    for part in range(2):
        arrive(from_opposite[part])
        for d in y_steps:
            for c in range(2):
                where = device(x, y + d, z, core + c * twin)
                rest.append(send_acts(other, part, where, at_y(4 - d, 1 - half) + c * twin))
        rest.append(send_acts(other, part, partner, other + twin))
        if part == 0:
            for d in (1, 2, 3):
                start(
                    ("z", d),
                    remote(
                        far_piece(0), far_piece(0), zg_ss.at[d - 1], zg_rs.at[d - 1], z_peers[d - 1]
                    ),
                )
    for d in (1, 2, 3):
        arrive(("z", d))
        spread_x(d)
    for key in rest:
        arrive(key)
    pre[...] = (
        jnp.dot(
            project_t[...],
            acts[...].reshape(MEMBERS * 4 * OWN, LANES),
            preferred_element_type=F32,
        )
        + columns[:, 0:1]
    )
    head_grad = jnp.where(pre[...] > 0, cot_t[...], 0.0).astype(BF16)
    branch_grads = []
    for block in (member, other):
        act_grad = jnp.dot(
            project[block].reshape(4 * OWN, OUTPUTS), head_grad, preferred_element_type=F32
        )
        branch_grads.append(jnp.where(acts[block] > 0, act_grad, 0.0).astype(BF16))
    for k in (3, 2, 1, 0):
        for side in range(2):
            grads[k, pl.ds(side * OWN, OWN), :] = branch_grads[side][k * OWN:(k + 1) * OWN]
        for slot in (2 * k - 2, 2 * k - 1) if k else ():
            start(
                ("grad", slot),
                remote(
                    grads.at[k], grad_recv.at[slot], grow_ss.at[slot], grow_rs.at[slot],
                    (row + row_offset(slot), member),
                ),
                sends(slot),
                gets(slot),
            )
    own_head = jnp.maximum(pre[pl.ds(pl.multiple_of(member * OWN, OWN), OWN), :], 0.0)
    for r in range(HEIGHT):
        head_ref[r] = own_head[:, r * BREADTH:(r + 1) * BREADTH].astype(BF16)

    def put(values, t):
        low = values.astype(BF16)
        for side in range(2):
            spread[pl.ds(side * TERMS + t * OWN, OWN), :] = low[side * OWN:(side + 1) * OWN]

    def put_columns(field, k, i):
        for j in range(3):
            put(shift_columns(field, -(j - 1) * DILATIONS[k]), 9 * k + 3 * i + j)

    put(grads[0].astype(F32), TAPS - 1)
    for k in range(3):
        put_columns(grads[k + 1].astype(F32), k, 1)
    for k in range(3):
        for slot, i in ((2 * k, 2), (2 * k + 1, 0)):
            arrive(("grad", slot))
            put_columns(jnp.where(gets(slot), grad_recv[slot].astype(F32), 0.0), k, i)
    spread_t[...] = spread[...].T

    for block in range(4):
        loaded(("fill", block))
    for d in range(4):
        for e in (1, 2, 3):
            arrive(("x", d, e))
    def multiply(pair):
        product = jnp.dot(
            spread_t[pl.ds(0, PIXELS), :],
            w_both[:, pl.ds(pair * 512, 512)],
            preferred_element_type=F32,
        )
        for n in (2 * pair, 2 * pair + 1):
            for c in range(2):
                lane = (n % 2) * 256 + c * BLOCK
                piece = product[:, lane:lane + BLOCK]
                part_sum[n, c] = piece
                part_low[n, c] = piece.astype(BF16)
            start(
                ("core", n),
                remote(
                    part_low.at[n, 1 - core], core_recv.at[n], core_ss.at[n], core_rs.at[n],
                    partner,
                ),
            )

    def send_sum(n):
        arrive(("core", n))
        sum_send[n] = (part_sum[n, core] + core_recv[n].astype(F32)).astype(BF16)
        start(
            ("sum", n),
            remote(
                sum_send.at[n], sum_recv.at[n], sum_ss.at[n], sum_rs.at[n],
                device(x, y + order[n], z, core),
            ),
        )

    multiply(0)
    multiply(1)
    for n in range(3):
        send_sum(n)
    drain()
    arrive(("core", 3))
    total = part_sum[3, core] + core_recv[3].astype(F32)
    for n in (1, 2, 0):
        arrive(("sum", n))
        total = total + sum_recv[n].astype(F32)
    grad_ref[...] = total.astype(BF16)
    finish()


def hand_out(head_in, grad_in, head_out, grad_out, sems):
    copies = [
        pltpu.make_async_copy(head_in, head_out, sems.at[0]),
        pltpu.make_async_copy(grad_in, grad_out, sems.at[1]),
    ]
    for copy in copies:
        copy.start()
    for copy in copies:
        copy.wait()


def on_device(
    features, point_weight, dilated_weight, branch_bias, project_weight, project_bias, cotangent
):
    in_place = pl.BlockSpec(memory_space=pltpu.HBM)
    vmem = pl.BlockSpec(memory_space=pltpu.VMEM)
    dma = pltpu.SemaphoreType.DMA
    head, grad = pl.pallas_call(
        kernel,
        out_shape=(
            pltpu.VMEM((HEIGHT, OWN, BREADTH), BF16),
            pltpu.VMEM((PIXELS, BLOCK), BF16),
        ),
        in_specs=[in_place] * 7,
        out_specs=(vmem, vmem),
        scratch_shapes=[
            pltpu.VMEM((4, OWN), F32),
            pltpu.VMEM((1, OUTPUTS), F32),
            pltpu.VMEM((LANES, CHANNELS), BF16),
            pltpu.VMEM((TERMS, CHANNELS), BF16),
            pltpu.VMEM((2 * TERMS, CHANNELS // 2), BF16),
            pltpu.VMEM((MEMBERS, 4, OWN, OUTPUTS), BF16),
            pltpu.VMEM((OUTPUTS, MEMBERS * 4 * OWN), BF16),
            pltpu.VMEM((LANES, OUTPUTS), BF16),
            pltpu.VMEM((OUTPUTS, LANES), F32),
            pltpu.VMEM((OUTPUTS, BLOCK), F32),
            pltpu.VMEM((TERMS, LANES), F32),
            pltpu.VMEM((6, OWN, LANES), F32),
            pltpu.VMEM((6, OWN, LANES), F32),
            pltpu.VMEM((MEMBERS, 4 * OWN, LANES), BF16),
            pltpu.VMEM((OUTPUTS, LANES), F32),
            pltpu.VMEM((4, 2 * OWN, LANES), BF16),
            pltpu.VMEM((6, 2 * OWN, LANES), BF16),
            pltpu.VMEM((2 * TERMS, LANES), BF16),
            pltpu.VMEM((LANES, 2 * TERMS), BF16),
            pltpu.VMEM((4, 2, PIXELS, BLOCK), F32),
            pltpu.VMEM((4, 2, PIXELS, BLOCK), BF16),
            pltpu.VMEM((4, PIXELS, BLOCK), BF16),
            pltpu.VMEM((3, PIXELS, BLOCK), BF16),
            pltpu.VMEM((3, PIXELS, BLOCK), BF16),
            pltpu.SemaphoreType.REGULAR((1,)),
            dma((13,)), dma((4,)), dma((6,)), dma((6,)), dma((23,)), dma((16, 2)),
            dma((1,)), dma((1,)), dma((3,)), dma((3,)), dma((12,)), dma((12,)),
            dma((6,)), dma((6,)), dma((4,)), dma((4,)), dma((3,)), dma((3,)),
        ],
        compiler_params=pltpu.CompilerParams(
            collective_id=0, has_side_effects=True, vmem_limit_bytes=58 * 1024 * 1024
        ),
        name="pyramid",
    )(
        features.reshape(PIXELS, CHANNELS),
        jnp.transpose(dilated_weight, (0, 1, 2, 4, 3)).reshape(TERMS - OWN, CHANNELS),
        point_weight.T,
        project_weight.reshape(4, MEMBERS, OWN, OUTPUTS),
        cotangent.reshape(PIXELS, OUTPUTS),
        branch_bias,
        project_bias.reshape(1, OUTPUTS),
    )
    head, grad = pl.pallas_call(
        hand_out,
        out_shape=(
            jax.ShapeDtypeStruct((HEIGHT, OWN, BREADTH), BF16),
            jax.ShapeDtypeStruct((PIXELS, BLOCK), BF16),
        ),
        in_specs=[vmem] * 2,
        out_specs=(in_place, in_place),
        scratch_shapes=[dma((2,))],
        name="hand_out",
    )(*[pltpu.with_memory_space_constraint(value, pltpu.VMEM) for value in (head, grad)])
    return (jnp.transpose(head, (0, 2, 1)), grad.reshape(HEIGHT, BREADTH, BLOCK))


def solution(mesh):
    in_specs = (
        P("rows", None, None),
        P(None, "filt"),
        P(None, None, None, None, "filt"),
        P(None, "filt"),
        P(),
        P(),
        P("rows", None, None),
    )
    out_specs = (P("rows", None, "filt"), P("rows", None, "filt"))
    return jax.shard_map(
        on_device, mesh=mesh, in_specs=in_specs, out_specs=out_specs, check_vma=False
    )
```

```python
import jax
import jax.numpy as jnp
from jax import lax
from jax.experimental import pallas as pl
from jax.experimental.pallas import tpu as pltpu
from jax.sharding import PartitionSpec as P

FIRST_DILATION = 12
SECOND_DILATION = 24
THIRD_DILATION = 36
DILATIONS = (FIRST_DILATION, SECOND_DILATION, THIRD_DILATION)
ROW_BLOCKS = 64
HEIGHT = 12
BREADTH = 48
PIXELS = HEIGHT * BREADTH
LANES = 640
CHANNELS = 2048
OWN = 16
TAPS = 28
TERMS = TAPS * OWN
MEMBERS = 16
OUTPUTS = 256
BLOCK = 128
PIECE_ROWS = TERMS // 4
PIECE_LANES = 256
MESH = pl.DeviceIdType.MESH
BF16 = jnp.bfloat16
F32 = jnp.float32


def device(x, y, z, core):
    x, y, z = lax.rem(x + 4, 4), lax.rem(y + 4, 4), lax.rem(z + 32, 32)
    return (lax.rem(z, 16) * 4 + x, (y * 2 + z // 16) * 2 + core)


def remote(source, target, send_sem, recv_sem, where):
    return pltpu.make_async_remote_copy(
        src_ref=source,
        dst_ref=target,
        send_sem=send_sem,
        recv_sem=recv_sem,
        device_id=where,
        device_id_type=MESH,
    )


def kernel(
    x_hbm, dilated_hbm, point_hbm, project_hbm, cot_hbm, bias_hbm, project_bias_hbm,
    head_ref, grad_ref,
    bias_ref, project_bias_ref, x_buf, w_buf, w_both, project, project_t, cot_buf, cot_t, columns,
    taps, row_send, row_recv, acts, pre, grads, grad_recv, spread, spread_t,
    part_sum, part_low, core_recv, sum_send, sum_recv,
    far, load_sem, fill_sem, row_ss, row_rs, act_ss, act_rs, first_ss, first_rs, zg_ss, zg_rs,
    xg_ss, xg_rs, grow_ss, grow_rs, core_ss, core_rs, sum_ss, sum_rs,
):
    row = lax.axis_index("rows")
    member = lax.axis_index("filt")
    x, z_low = lax.rem(row, 4), row // 4
    y, half, core = member // 4, lax.rem(member // 2, 2), lax.rem(member, 2)
    z = half * 16 + z_low
    z_quarter = lax.rem(z_low, 4)
    other = member + 2 - 4 * half
    twin = 1 - 2 * core

    def row_offset(slot):
        return (slot // 2 + 1) * (1 - 2 * (slot % 2))

    def sends(slot):
        place = row + row_offset(slot)
        return jnp.logical_and(place >= 0, place < ROW_BLOCKS)

    def gets(slot):
        place = row - row_offset(slot)
        return jnp.logical_and(place >= 0, place < ROW_BLOCKS)

    opposite = device(x, y, z + 16, core)
    group = z_low // 4
    outer = jnp.logical_or(group == 0, group == 3)
    inner = jnp.logical_not(outer)
    inward = jnp.where(group < 2, 4, -4)
    z_outward, z_inward = device(x, y, z - inward, core), device(x, y, z + inward, core)
    partner = device(x, y, z, 1 - core)
    y_steps = (2, 1, 3)
    z_ahead, z_behind = device(x, y, z + 8, core), device(x, y, z - 8, core)

    def at_y(step, side):
        return (lax.rem(y + step, 4) * 2 + side) * 2 + core

    z_base = z - z_quarter
    z_peers = [device(x, y, z_base + lax.rem(z_quarter + d, 4), core) for d in (1, 2, 3)]
    x_peers = [device(x + d, y, z, core) for d in (1, 2, 3)]

    sent, due = [], {}

    def start(key, copy, gives=None, takes=None):
        sent.append((copy, gives))
        due[key] = (copy, takes)
        if gives is None:
            copy.start()
        else:
            pl.when(gives)(copy.start)

    def arrive(key):
        copy, takes = due.pop(key)
        if takes is None:
            copy.wait_recv()
        else:
            pl.when(takes)(copy.wait_recv)

    def drain():
        for copy, gives in sent:
            if gives is None:
                copy.wait_send()
            else:
                pl.when(gives)(copy.wait_send)
        sent.clear()

    def finish():
        for key in list(due):
            arrive(key)
        drain()
        for load in list(loading):
            loaded(load)

    loading = {}

    def load(key, source, target, sem):
        loading[key] = pltpu.make_async_copy(source, target, sem)
        loading[key].start()

    def loaded(key):
        loading.pop(key).wait()

    barrier = pltpu.get_barrier_semaphore()
    fixed_peers = (
        [z_ahead, z_behind, z_outward, z_inward, partner] + z_peers + x_peers
        + [device(x, y + d, z, c) for d in y_steps for c in range(2)]
    )
    for peer in fixed_peers:
        pl.semaphore_signal(barrier, inc=1, device_id=peer, device_id_type=MESH)
    heard = jnp.int32(len(fixed_peers))
    for slot in range(6):
        @pl.when(sends(slot))
        def _():
            pl.semaphore_signal(
                barrier, inc=1, device_id=(row + row_offset(slot), member), device_id_type=MESH
            )
        heard = heard + sends(slot).astype(jnp.int32)

    halves = [pl.ds(n * (CHANNELS // 2), CHANNELS // 2) for n in range(2)]
    for n in range(2):
        load(
            ("x", n), x_hbm.at[:, halves[n]], x_buf.at[pl.ds(0, PIXELS), halves[n]], load_sem.at[n]
        )
        load(
            ("w", n),
            dilated_hbm.at[:, halves[n]],
            w_buf.at[pl.ds(0, TERMS - OWN), halves[n]],
            load_sem.at[2 + n],
        )
        load(
            ("p", n),
            point_hbm.at[:, halves[n]],
            w_buf.at[pl.ds(TERMS - OWN, OWN), halves[n]],
            load_sem.at[4 + n],
        )
    load("bias", bias_hbm, bias_ref, load_sem.at[6])
    load("cot", cot_hbm, cot_buf.at[pl.ds(0, PIXELS)], load_sem.at[7])
    for k in range(4):
        load(("project", k), project_hbm.at[k], project.at[:, k], load_sem.at[8 + k])
    load("project_bias", project_bias_hbm, project_bias_ref, load_sem.at[12])
    x_buf[pl.ds(PIXELS, LANES - PIXELS), :] = jnp.zeros((LANES - PIXELS, CHANNELS), BF16)
    cot_buf[pl.ds(PIXELS, LANES - PIXELS), :] = jnp.zeros((LANES - PIXELS, OUTPUTS), BF16)
    for n in range(2):
        for key in ("x", "w", "p"):
            loaded((key, n))
        product = lax.dot_general(
            w_buf[:, halves[n]],
            x_buf[:, halves[n]],
            (((1,), (1,)), ((), ())),
            preferred_element_type=F32,
        )
        taps[...] = product if n == 0 else taps[...] + product
    order = (2, 1, 3, 0)
    for n in range(4):
        lanes = pl.multiple_of(lax.rem(y + order[n], 4) * 512 + half * 256, 256)
        load(
            ("fill", n),
            w_buf.at[:, pl.ds(lanes, 256)],
            w_both.at[pl.ds(0, TERMS), pl.ds(n * 256, 256)],
            fill_sem.at[n],
        )
    column = lax.rem(lax.broadcasted_iota(jnp.int32, (1, LANES), 1), BREADTH)

    def shift_columns(field, amount):
        if amount == 0:
            return field
        inside = jnp.logical_and(column + amount >= 0, column + amount < BREADTH)
        return jnp.where(inside, pltpu.roll(field, (-amount) % LANES, 1), 0.0)

    def tap(k, i, j):
        return taps[pl.ds((9 * k + 3 * i + j) * OWN, OWN), :]

    def row_sum(k, i):
        d = DILATIONS[k]
        return (
            shift_columns(tap(k, i, 0), -d) + tap(k, i, 1) + shift_columns(tap(k, i, 2), d)
        )

    for k in range(3):
        row_send[2 * k] = row_sum(k, 0)
        row_send[2 * k + 1] = row_sum(k, 2)
    pl.semaphore_wait(barrier, heard)
    pl.semaphore_signal(far.at[0], inc=1, device_id=z_ahead, device_id_type=MESH)
    for slot in (4, 5, 2, 3, 0, 1):
        start(
            ("row", slot),
            remote(
                row_send.at[slot], row_recv.at[slot], row_ss.at[slot], row_rs.at[slot],
                (row + row_offset(slot), member),
            ),
            sends(slot),
            gets(slot),
        )

    z_rows = pl.multiple_of(z_quarter * PIECE_ROWS, 16)
    far_rows = pl.multiple_of(TERMS + z_quarter * PIECE_ROWS, 16)
    far_lanes = pl.multiple_of(x * PIECE_LANES, 128)
    ahead = jnp.where(x == 0, 2, jnp.where(x == 1, 1, jnp.where(x == 2, 3, 0)))
    give_lanes = pl.multiple_of(lax.rem(y + ahead, 4) * 512 + (1 - half) * 256, 256)
    start(
        "give",
        remote(
            w_buf.at[pl.ds(z_rows, PIECE_ROWS), pl.ds(give_lanes, PIECE_LANES)],
            w_both.at[pl.ds(far_rows, PIECE_ROWS), pl.ds(far_lanes, PIECE_LANES)],
            first_ss.at[0], first_rs.at[0], z_outward,
        ),
        outer,
        outer,
    )

    def diagonal(values, size):
        same = lax.broadcasted_iota(jnp.int32, (size, size), 0) == lax.broadcasted_iota(
            jnp.int32, (size, size), 1
        )
        return jnp.sum(
            jnp.where(same, jnp.broadcast_to(values, (size, size)), 0.0), axis=1, keepdims=True
        )

    loaded("bias")
    bias = bias_ref[...]
    biases = [diagonal(bias[k:k + 1, :], OWN) for k in range(4)]
    acts[member, pl.ds(0, OWN), :] = jnp.maximum(
        taps[pl.ds(TERMS - OWN, OWN), :] + biases[0], 0.0
    ).astype(BF16)
    centres = [row_sum(k, 1) + biases[k + 1] for k in range(3)]

    def far_piece(d):
        rows_from = pl.multiple_of(
            TERMS + lax.rem(z_quarter + 4 - d, 4) * PIECE_ROWS, 16
        )
        return w_both.at[pl.ds(rows_from, PIECE_ROWS), pl.ds(far_lanes, PIECE_LANES)]

    def spread_x(d, where):
        for e in (1, 2, 3):
            n = 3 * d + e - 1
            start(
                ("x", where is outer, d, e),
                remote(far_piece(d), far_piece(d), xg_ss.at[n], xg_rs.at[n], x_peers[e - 1]),
                where,
                where,
            )

    def spread_z(where):
        for d in (1, 2, 3):
            start(
                ("z", where is outer, d),
                remote(
                    far_piece(0), far_piece(0), zg_ss.at[d - 1], zg_rs.at[d - 1], z_peers[d - 1]
                ),
                where,
                where,
            )

    def pass_z(where):
        for d in (1, 2, 3):
            arrive(("z", where is outer, d))
            spread_x(d, where)

    arrive("give")
    spread_x(0, outer)

    def send_acts(block, part, where, arriving):
        n = len(passed)
        passed.append(block)
        rows = pl.ds(0, 4 * OWN) if part is None else pl.ds(part * 2 * OWN, 2 * OWN)
        place = 0 if part is None else part

        def copy(of):
            ref = acts.at[of, rows]
            return remote(ref, ref, act_ss.at[n], act_rs.at[of, place], where)

        start(("act", n), copy(block))
        due[("act", n)] = (copy(arriving), None)
        return ("act", n)

    passed = []
    for k in range(3):
        total = centres[k]
        for slot in (2 * k, 2 * k + 1):
            arrive(("row", slot))
            total = total + jnp.where(gets(slot), row_recv[slot], 0.0)
        acts[member, pl.ds((k + 1) * OWN, OWN), :] = jnp.maximum(total, 0.0).astype(BF16)
    pl.semaphore_wait(far.at[0], 1)
    from_opposite = [send_acts(member, part, opposite, other) for part in range(2)]
    own_y = {}
    for d in y_steps:
        own_y[4 - d] = send_acts(
            member, None, device(x, y + d, z, core), at_y(4 - d, half)
        )
    rest = [send_acts(member, None, partner, member + twin)]

    for k in range(4):
        loaded(("project", k))
    loaded("cot")
    loaded("project_bias")
    project_t[...] = project[...].reshape(MEMBERS * 4 * OWN, OUTPUTS).T
    cot_t[...] = cot_buf[...].astype(F32).T
    columns[...] = jnp.broadcast_to(diagonal(project_bias_ref[...], OUTPUTS), (OUTPUTS, BLOCK))
    for d in (1, 3, 2):
        arrive(own_y[d])
        block = at_y(d, half)
        rest.append(send_acts(block, None, partner, block + twin))
    for part in range(2):
        arrive(from_opposite[part])
        for d in y_steps:
            for c in range(2):
                where = device(x, y + d, z, core + c * twin)
                rest.append(send_acts(other, part, where, at_y(4 - d, 1 - half) + c * twin))
        rest.append(send_acts(other, part, partner, other + twin))
        if part == 0:
            start(
                "relay",
                remote(far_piece(0), far_piece(0), first_ss.at[1], first_rs.at[1], z_inward),
                outer,
                inner,
            )
            spread_z(outer)
    arrive("relay")
    spread_z(inner)
    spread_x(0, inner)
    pass_z(outer)
    for key in rest:
        arrive(key)
    pre[...] = (
        jnp.dot(
            project_t[...],
            acts[...].reshape(MEMBERS * 4 * OWN, LANES),
            preferred_element_type=F32,
        )
        + columns[:, 0:1]
    )
    head_grad = jnp.where(pre[...] > 0, cot_t[...], 0.0).astype(BF16)
    branch_grads = []
    for block in (member, other):
        act_grad = jnp.dot(
            project[block].reshape(4 * OWN, OUTPUTS), head_grad, preferred_element_type=F32
        )
        branch_grads.append(jnp.where(acts[block] > 0, act_grad, 0.0).astype(BF16))
    for k in (3, 2, 1, 0):
        for side in range(2):
            grads[k, pl.ds(side * OWN, OWN), :] = branch_grads[side][k * OWN:(k + 1) * OWN]
        for slot in (2 * k - 2, 2 * k - 1) if k else ():
            start(
                ("grad", slot),
                remote(
                    grads.at[k], grad_recv.at[slot], grow_ss.at[slot], grow_rs.at[slot],
                    (row + row_offset(slot), member),
                ),
                sends(slot),
                gets(slot),
            )
    pass_z(inner)

    own_head = jnp.maximum(pre[pl.ds(pl.multiple_of(member * OWN, OWN), OWN), :], 0.0)
    for r in range(HEIGHT):
        head_ref[r] = own_head[:, r * BREADTH:(r + 1) * BREADTH].astype(BF16)

    def put(values, t):
        low = values.astype(BF16)
        for side in range(2):
            spread[pl.ds(side * TERMS + t * OWN, OWN), :] = low[side * OWN:(side + 1) * OWN]

    def put_columns(field, k, i):
        for j in range(3):
            put(shift_columns(field, -(j - 1) * DILATIONS[k]), 9 * k + 3 * i + j)

    put(grads[0].astype(F32), TAPS - 1)
    for k in range(3):
        put_columns(grads[k + 1].astype(F32), k, 1)
    for k in range(3):
        for slot, i in ((2 * k, 2), (2 * k + 1, 0)):
            arrive(("grad", slot))
            put_columns(jnp.where(gets(slot), grad_recv[slot].astype(F32), 0.0), k, i)
    spread_t[...] = spread[...].T

    for block in range(4):
        loaded(("fill", block))
    for d in range(4):
        for e in (1, 2, 3):
            arrive(("x", True, d, e))
            arrive(("x", False, d, e))
    def multiply(pair):
        product = jnp.dot(
            spread_t[pl.ds(0, PIXELS), :],
            w_both[:, pl.ds(pair * 512, 512)],
            preferred_element_type=F32,
        )
        for n in (2 * pair, 2 * pair + 1):
            for c in range(2):
                lane = (n % 2) * 256 + c * BLOCK
                piece = product[:, lane:lane + BLOCK]
                part_sum[n, c] = piece
                part_low[n, c] = piece.astype(BF16)
            start(
                ("core", n),
                remote(
                    part_low.at[n, 1 - core], core_recv.at[n], core_ss.at[n], core_rs.at[n],
                    partner,
                ),
            )

    def send_sum(n):
        arrive(("core", n))
        sum_send[n] = (part_sum[n, core] + core_recv[n].astype(F32)).astype(BF16)
        start(
            ("sum", n),
            remote(
                sum_send.at[n], sum_recv.at[n], sum_ss.at[n], sum_rs.at[n],
                device(x, y + order[n], z, core),
            ),
        )

    multiply(0)
    multiply(1)
    for n in range(3):
        send_sum(n)
    drain()
    arrive(("core", 3))
    total = part_sum[3, core] + core_recv[3].astype(F32)
    for n in (1, 2, 0):
        arrive(("sum", n))
        total = total + sum_recv[n].astype(F32)
    grad_ref[...] = total.astype(BF16)
    finish()


def hand_out(head_in, grad_in, head_out, grad_out, sems):
    copies = [
        pltpu.make_async_copy(head_in, head_out, sems.at[0]),
        pltpu.make_async_copy(grad_in, grad_out, sems.at[1]),
    ]
    for copy in copies:
        copy.start()
    for copy in copies:
        copy.wait()


def on_device(
    features, point_weight, dilated_weight, branch_bias, project_weight, project_bias, cotangent
):
    in_place = pl.BlockSpec(memory_space=pltpu.HBM)
    vmem = pl.BlockSpec(memory_space=pltpu.VMEM)
    dma = pltpu.SemaphoreType.DMA
    head, grad = pl.pallas_call(
        kernel,
        out_shape=(
            pltpu.VMEM((HEIGHT, OWN, BREADTH), BF16),
            pltpu.VMEM((PIXELS, BLOCK), BF16),
        ),
        in_specs=[in_place] * 7,
        out_specs=(vmem, vmem),
        scratch_shapes=[
            pltpu.VMEM((4, OWN), F32),
            pltpu.VMEM((1, OUTPUTS), F32),
            pltpu.VMEM((LANES, CHANNELS), BF16),
            pltpu.VMEM((TERMS, CHANNELS), BF16),
            pltpu.VMEM((2 * TERMS, CHANNELS // 2), BF16),
            pltpu.VMEM((MEMBERS, 4, OWN, OUTPUTS), BF16),
            pltpu.VMEM((OUTPUTS, MEMBERS * 4 * OWN), BF16),
            pltpu.VMEM((LANES, OUTPUTS), BF16),
            pltpu.VMEM((OUTPUTS, LANES), F32),
            pltpu.VMEM((OUTPUTS, BLOCK), F32),
            pltpu.VMEM((TERMS, LANES), F32),
            pltpu.VMEM((6, OWN, LANES), F32),
            pltpu.VMEM((6, OWN, LANES), F32),
            pltpu.VMEM((MEMBERS, 4 * OWN, LANES), BF16),
            pltpu.VMEM((OUTPUTS, LANES), F32),
            pltpu.VMEM((4, 2 * OWN, LANES), BF16),
            pltpu.VMEM((6, 2 * OWN, LANES), BF16),
            pltpu.VMEM((2 * TERMS, LANES), BF16),
            pltpu.VMEM((LANES, 2 * TERMS), BF16),
            pltpu.VMEM((4, 2, PIXELS, BLOCK), F32),
            pltpu.VMEM((4, 2, PIXELS, BLOCK), BF16),
            pltpu.VMEM((4, PIXELS, BLOCK), BF16),
            pltpu.VMEM((3, PIXELS, BLOCK), BF16),
            pltpu.VMEM((3, PIXELS, BLOCK), BF16),
            pltpu.SemaphoreType.REGULAR((1,)),
            dma((13,)), dma((4,)), dma((6,)), dma((6,)), dma((23,)), dma((16, 2)),
            dma((2,)), dma((2,)), dma((3,)), dma((3,)), dma((12,)), dma((12,)),
            dma((6,)), dma((6,)), dma((4,)), dma((4,)), dma((3,)), dma((3,)),
        ],
        compiler_params=pltpu.CompilerParams(
            collective_id=0, has_side_effects=True, vmem_limit_bytes=58 * 1024 * 1024
        ),
        name="pyramid",
    )(
        features.reshape(PIXELS, CHANNELS),
        jnp.transpose(dilated_weight, (0, 1, 2, 4, 3)).reshape(TERMS - OWN, CHANNELS),
        point_weight.T,
        project_weight.reshape(4, MEMBERS, OWN, OUTPUTS),
        cotangent.reshape(PIXELS, OUTPUTS),
        branch_bias,
        project_bias.reshape(1, OUTPUTS),
    )
    head, grad = pl.pallas_call(
        hand_out,
        out_shape=(
            jax.ShapeDtypeStruct((HEIGHT, OWN, BREADTH), BF16),
            jax.ShapeDtypeStruct((PIXELS, BLOCK), BF16),
        ),
        in_specs=[vmem] * 2,
        out_specs=(in_place, in_place),
        scratch_shapes=[dma((2,))],
        name="hand_out",
    )(*[pltpu.with_memory_space_constraint(value, pltpu.VMEM) for value in (head, grad)])
    return (jnp.transpose(head, (0, 2, 1)), grad.reshape(HEIGHT, BREADTH, BLOCK))


def solution(mesh):
    in_specs = (
        P("rows", None, None),
        P(None, "filt"),
        P(None, None, None, None, "filt"),
        P(None, "filt"),
        P(),
        P(),
        P("rows", None, None),
    )
    out_specs = (P("rows", None, "filt"), P("rows", None, "filt"))
    return jax.shard_map(
        on_device, mesh=mesh, in_specs=in_specs, out_specs=out_specs, check_vma=False
    )
```

```python
import jax
import jax.numpy as jnp
from jax import lax
from jax.experimental import pallas as pl
from jax.experimental.pallas import tpu as pltpu
from jax.sharding import PartitionSpec as P

FIRST_DILATION = 12
SECOND_DILATION = 24
THIRD_DILATION = 36
DILATIONS = (FIRST_DILATION, SECOND_DILATION, THIRD_DILATION)
ROW_BLOCKS = 64
HEIGHT = 12
BREADTH = 48
PIXELS = HEIGHT * BREADTH
LANES = 640
CHANNELS = 2048
OWN = 16
TAPS = 28
TERMS = TAPS * OWN
MEMBERS = 16
OUTPUTS = 256
BLOCK = 128
PIECE_ROWS = TERMS // 4
PIECE_LANES = 256
MESH = pl.DeviceIdType.MESH
BF16 = jnp.bfloat16
F32 = jnp.float32


def device(x, y, z, core):
    x, y, z = lax.rem(x + 4, 4), lax.rem(y + 4, 4), lax.rem(z + 32, 32)
    return (lax.rem(z, 16) * 4 + x, (y * 2 + z // 16) * 2 + core)


def remote(source, target, send_sem, recv_sem, where):
    return pltpu.make_async_remote_copy(
        src_ref=source,
        dst_ref=target,
        send_sem=send_sem,
        recv_sem=recv_sem,
        device_id=where,
        device_id_type=MESH,
    )


def kernel(
    x_hbm, dilated_hbm, point_hbm, project_hbm, cot_hbm, bias_hbm, project_bias_hbm,
    head_ref, grad_ref,
    bias_ref, project_bias_ref, x_buf, w_buf, w_both, project, project_t, cot_buf, cot_t, columns,
    taps, row_send, row_recv, acts, pre, grads, grad_recv, spread, spread_t,
    part_sum, part_low, core_recv, sum_send, sum_recv,
    far, load_sem, fill_sem, row_ss, row_rs, act_ss, act_rs, first_ss, first_rs, zg_ss, zg_rs,
    xg_ss, xg_rs, grow_ss, grow_rs, core_ss, core_rs, sum_ss, sum_rs,
):
    row = lax.axis_index("rows")
    member = lax.axis_index("filt")
    x, z_low = lax.rem(row, 4), row // 4
    y, half, core = member // 4, lax.rem(member // 2, 2), lax.rem(member, 2)
    z = half * 16 + z_low
    z_quarter = lax.rem(z_low, 4)
    other = member + 2 - 4 * half
    twin = 1 - 2 * core

    def row_offset(slot):
        return (slot // 2 + 1) * (1 - 2 * (slot % 2))

    def sends(slot):
        place = row + row_offset(slot)
        return jnp.logical_and(place >= 0, place < ROW_BLOCKS)

    def gets(slot):
        place = row - row_offset(slot)
        return jnp.logical_and(place >= 0, place < ROW_BLOCKS)

    opposite = device(x, y, z + 16, core)
    group = z_low // 4
    outer = jnp.logical_or(group == 0, group == 3)
    inner = jnp.logical_not(outer)
    inward = jnp.where(group < 2, 4, -4)
    z_outward, z_inward = device(x, y, z - inward, core), device(x, y, z + inward, core)
    partner = device(x, y, z, 1 - core)
    y_steps = (2, 1, 3)
    z_ahead, z_behind = device(x, y, z + 8, core), device(x, y, z - 8, core)

    def at_y(step, side):
        return (lax.rem(y + step, 4) * 2 + side) * 2 + core

    z_base = z - z_quarter
    z_peers = [device(x, y, z_base + lax.rem(z_quarter + d, 4), core) for d in (1, 2, 3)]
    x_peers = [device(x + d, y, z, core) for d in (1, 2, 3)]

    sent, due = [], {}

    def start(key, copy, gives=None, takes=None):
        sent.append((copy, gives))
        due[key] = (copy, takes)
        if gives is None:
            copy.start()
        else:
            pl.when(gives)(copy.start)

    def arrive(key):
        copy, takes = due.pop(key)
        if takes is None:
            copy.wait_recv()
        else:
            pl.when(takes)(copy.wait_recv)

    def drain():
        for copy, gives in sent:
            if gives is None:
                copy.wait_send()
            else:
                pl.when(gives)(copy.wait_send)
        sent.clear()

    def finish():
        for key in list(due):
            arrive(key)
        drain()
        for load in list(loading):
            loaded(load)

    loading = {}

    def load(key, source, target, sem):
        loading[key] = pltpu.make_async_copy(source, target, sem)
        loading[key].start()

    def loaded(key):
        loading.pop(key).wait()

    barrier = pltpu.get_barrier_semaphore()
    fixed_peers = (
        [z_ahead, z_behind, z_outward, z_inward, partner] + z_peers + x_peers
        + [device(x, y + d, z, c) for d in y_steps for c in range(2)]
    )
    for peer in fixed_peers:
        pl.semaphore_signal(barrier, inc=1, device_id=peer, device_id_type=MESH)
    heard = jnp.int32(len(fixed_peers))
    for slot in range(6):
        @pl.when(sends(slot))
        def _():
            pl.semaphore_signal(
                barrier, inc=1, device_id=(row + row_offset(slot), member), device_id_type=MESH
            )
        heard = heard + sends(slot).astype(jnp.int32)

    halves = [pl.ds(n * (CHANNELS // 2), CHANNELS // 2) for n in range(2)]
    for n in range(2):
        load(
            ("x", n), x_hbm.at[:, halves[n]], x_buf.at[pl.ds(0, PIXELS), halves[n]], load_sem.at[n]
        )
        load(
            ("w", n),
            dilated_hbm.at[:, halves[n]],
            w_buf.at[pl.ds(0, TERMS - OWN), halves[n]],
            load_sem.at[2 + n],
        )
        load(
            ("p", n),
            point_hbm.at[:, halves[n]],
            w_buf.at[pl.ds(TERMS - OWN, OWN), halves[n]],
            load_sem.at[4 + n],
        )
    load("bias", bias_hbm, bias_ref, load_sem.at[6])
    load("cot", cot_hbm, cot_buf.at[pl.ds(0, PIXELS)], load_sem.at[7])
    for k in range(4):
        load(("project", k), project_hbm.at[k], project.at[:, k], load_sem.at[8 + k])
    load("project_bias", project_bias_hbm, project_bias_ref, load_sem.at[12])
    x_buf[pl.ds(PIXELS, LANES - PIXELS), :] = jnp.zeros((LANES - PIXELS, CHANNELS), BF16)
    cot_buf[pl.ds(PIXELS, LANES - PIXELS), :] = jnp.zeros((LANES - PIXELS, OUTPUTS), BF16)
    for n in range(2):
        for key in ("x", "w", "p"):
            loaded((key, n))
        product = lax.dot_general(
            w_buf[:, halves[n]],
            x_buf[:, halves[n]],
            (((1,), (1,)), ((), ())),
            preferred_element_type=F32,
        )
        taps[...] = product if n == 0 else taps[...] + product
    order = (2, 1, 3, 0)
    for n in range(4):
        lanes = pl.multiple_of(lax.rem(y + order[n], 4) * 512 + half * 256, 256)
        load(
            ("fill", n),
            w_buf.at[:, pl.ds(lanes, 256)],
            w_both.at[pl.ds(0, TERMS), pl.ds(n * 256, 256)],
            fill_sem.at[n],
        )
    column = lax.rem(lax.broadcasted_iota(jnp.int32, (1, LANES), 1), BREADTH)

    def shift_columns(field, amount):
        if amount == 0:
            return field
        inside = jnp.logical_and(column + amount >= 0, column + amount < BREADTH)
        return jnp.where(inside, pltpu.roll(field, (-amount) % LANES, 1), 0.0)

    def tap(k, i, j):
        return taps[pl.ds((9 * k + 3 * i + j) * OWN, OWN), :]

    def row_sum(k, i):
        d = DILATIONS[k]
        return (
            shift_columns(tap(k, i, 0), -d) + tap(k, i, 1) + shift_columns(tap(k, i, 2), d)
        )

    for k in range(3):
        row_send[2 * k] = row_sum(k, 0)
        row_send[2 * k + 1] = row_sum(k, 2)
    pl.semaphore_wait(barrier, heard)
    pl.semaphore_signal(far.at[0], inc=1, device_id=z_ahead, device_id_type=MESH)
    for slot in (4, 5, 2, 3, 0, 1):
        start(
            ("row", slot),
            remote(
                row_send.at[slot], row_recv.at[slot], row_ss.at[slot], row_rs.at[slot],
                (row + row_offset(slot), member),
            ),
            sends(slot),
            gets(slot),
        )

    z_rows = pl.multiple_of(z_quarter * PIECE_ROWS, 16)
    far_rows = pl.multiple_of(TERMS + z_quarter * PIECE_ROWS, 16)
    far_lanes = pl.multiple_of(x * PIECE_LANES, 128)
    ahead = jnp.where(x == 0, 2, jnp.where(x == 1, 1, jnp.where(x == 2, 3, 0)))
    give_lanes = pl.multiple_of(lax.rem(y + ahead, 4) * 512 + (1 - half) * 256, 256)
    start(
        "give",
        remote(
            w_buf.at[pl.ds(z_rows, PIECE_ROWS), pl.ds(give_lanes, PIECE_LANES)],
            w_both.at[pl.ds(far_rows, PIECE_ROWS), pl.ds(far_lanes, PIECE_LANES)],
            first_ss.at[0], first_rs.at[0], z_outward,
        ),
        outer,
        outer,
    )

    def diagonal(values, size):
        same = lax.broadcasted_iota(jnp.int32, (size, size), 0) == lax.broadcasted_iota(
            jnp.int32, (size, size), 1
        )
        return jnp.sum(
            jnp.where(same, jnp.broadcast_to(values, (size, size)), 0.0), axis=1, keepdims=True
        )

    loaded("bias")
    bias = bias_ref[...]
    biases = [diagonal(bias[k:k + 1, :], OWN) for k in range(4)]
    acts[member, pl.ds(0, OWN), :] = jnp.maximum(
        taps[pl.ds(TERMS - OWN, OWN), :] + biases[0], 0.0
    ).astype(BF16)
    centres = [row_sum(k, 1) + biases[k + 1] for k in range(3)]

    def far_piece(d):
        rows_from = pl.multiple_of(
            TERMS + lax.rem(z_quarter + 4 - d, 4) * PIECE_ROWS, 16
        )
        return w_both.at[pl.ds(rows_from, PIECE_ROWS), pl.ds(far_lanes, PIECE_LANES)]

    def spread_x(d, where):
        for e in (1, 2, 3):
            n = 3 * d + e - 1
            start(
                ("x", where is outer, d, e),
                remote(far_piece(d), far_piece(d), xg_ss.at[n], xg_rs.at[n], x_peers[e - 1]),
                where,
                where,
            )

    def spread_z(where):
        for d in (1, 2, 3):
            start(
                ("z", where is outer, d),
                remote(
                    far_piece(0), far_piece(0), zg_ss.at[d - 1], zg_rs.at[d - 1], z_peers[d - 1]
                ),
                where,
                where,
            )

    def pass_z(where):
        for d in (1, 2, 3):
            arrive(("z", where is outer, d))
            spread_x(d, where)

    arrive("give")
    spread_x(0, outer)

    def send_acts(block, part, where, arriving):
        n = len(passed)
        passed.append(block)
        rows = pl.ds(0, 4 * OWN) if part is None else pl.ds(part * 2 * OWN, 2 * OWN)
        place = 0 if part is None else part

        def copy(of):
            ref = acts.at[of, rows]
            return remote(ref, ref, act_ss.at[n], act_rs.at[of, place], where)

        start(("act", n), copy(block))
        due[("act", n)] = (copy(arriving), None)
        return ("act", n)

    passed = []
    for k in range(3):
        total = centres[k]
        for slot in (2 * k, 2 * k + 1):
            arrive(("row", slot))
            total = total + jnp.where(gets(slot), row_recv[slot], 0.0)
        acts[member, pl.ds((k + 1) * OWN, OWN), :] = jnp.maximum(total, 0.0).astype(BF16)
    pl.semaphore_wait(far.at[0], 1)
    from_opposite = [send_acts(member, part, opposite, other) for part in range(2)]
    own_y = {}
    for d in y_steps:
        own_y[4 - d] = send_acts(
            member, None, device(x, y + d, z, core), at_y(4 - d, half)
        )
    rest = [send_acts(member, None, partner, member + twin)]

    for k in range(4):
        loaded(("project", k))
    loaded("cot")
    loaded("project_bias")
    project_t[...] = project[...].reshape(MEMBERS * 4 * OWN, OUTPUTS).T
    cot_t[...] = cot_buf[...].astype(F32).T
    columns[...] = jnp.broadcast_to(diagonal(project_bias_ref[...], OUTPUTS), (OUTPUTS, BLOCK))
    for d in (1, 3, 2):
        arrive(own_y[d])
        block = at_y(d, half)
        rest.append(send_acts(block, None, partner, block + twin))
    for part in range(2):
        arrive(from_opposite[part])
        for d in y_steps:
            for c in range(2):
                where = device(x, y + d, z, core + c * twin)
                rest.append(send_acts(other, part, where, at_y(4 - d, 1 - half) + c * twin))
        rest.append(send_acts(other, part, partner, other + twin))
        if part == 0:
            start(
                "relay",
                remote(far_piece(0), far_piece(0), first_ss.at[1], first_rs.at[1], z_inward),
                outer,
                inner,
            )
            spread_z(outer)
    arrive("relay")
    spread_z(inner)
    spread_x(0, inner)
    pass_z(outer)
    for key in rest:
        arrive(key)
    pass_z(inner)
    pre[...] = (
        jnp.dot(
            project_t[...],
            acts[...].reshape(MEMBERS * 4 * OWN, LANES),
            preferred_element_type=F32,
        )
        + columns[:, 0:1]
    )
    head_grad = jnp.where(pre[...] > 0, cot_t[...], 0.0).astype(BF16)
    branch_grads = []
    for block in (member, other):
        act_grad = jnp.dot(
            project[block].reshape(4 * OWN, OUTPUTS), head_grad, preferred_element_type=F32
        )
        branch_grads.append(jnp.where(acts[block] > 0, act_grad, 0.0).astype(BF16))
    for k in (3, 2, 1, 0):
        for side in range(2):
            grads[k, pl.ds(side * OWN, OWN), :] = branch_grads[side][k * OWN:(k + 1) * OWN]
        for slot in (2 * k - 2, 2 * k - 1) if k else ():
            start(
                ("grad", slot),
                remote(
                    grads.at[k], grad_recv.at[slot], grow_ss.at[slot], grow_rs.at[slot],
                    (row + row_offset(slot), member),
                ),
                sends(slot),
                gets(slot),
            )

    own_head = jnp.maximum(pre[pl.ds(pl.multiple_of(member * OWN, OWN), OWN), :], 0.0)
    for r in range(HEIGHT):
        head_ref[r] = own_head[:, r * BREADTH:(r + 1) * BREADTH].astype(BF16)

    def put(values, t):
        low = values.astype(BF16)
        for side in range(2):
            spread[pl.ds(side * TERMS + t * OWN, OWN), :] = low[side * OWN:(side + 1) * OWN]

    def put_columns(field, k, i):
        for j in range(3):
            put(shift_columns(field, -(j - 1) * DILATIONS[k]), 9 * k + 3 * i + j)

    put(grads[0].astype(F32), TAPS - 1)
    for k in range(3):
        put_columns(grads[k + 1].astype(F32), k, 1)
    for k in range(3):
        for slot, i in ((2 * k, 2), (2 * k + 1, 0)):
            arrive(("grad", slot))
            put_columns(jnp.where(gets(slot), grad_recv[slot].astype(F32), 0.0), k, i)
    spread_t[...] = spread[...].T

    for block in range(4):
        loaded(("fill", block))
    for d in range(4):
        for e in (1, 2, 3):
            arrive(("x", True, d, e))
            arrive(("x", False, d, e))
    def multiply(pair):
        product = jnp.dot(
            spread_t[pl.ds(0, PIXELS), :],
            w_both[:, pl.ds(pair * 512, 512)],
            preferred_element_type=F32,
        )
        for n in (2 * pair, 2 * pair + 1):
            for c in range(2):
                lane = (n % 2) * 256 + c * BLOCK
                piece = product[:, lane:lane + BLOCK]
                part_sum[n, c] = piece
                part_low[n, c] = piece.astype(BF16)
            start(
                ("core", n),
                remote(
                    part_low.at[n, 1 - core], core_recv.at[n], core_ss.at[n], core_rs.at[n],
                    partner,
                ),
            )

    def send_sum(n):
        arrive(("core", n))
        sum_send[n] = (part_sum[n, core] + core_recv[n].astype(F32)).astype(BF16)
        start(
            ("sum", n),
            remote(
                sum_send.at[n], sum_recv.at[n], sum_ss.at[n], sum_rs.at[n],
                device(x, y + order[n], z, core),
            ),
        )

    multiply(0)
    multiply(1)
    for n in range(3):
        send_sum(n)
    drain()
    arrive(("core", 3))
    total = part_sum[3, core] + core_recv[3].astype(F32)
    for n in (1, 2, 0):
        arrive(("sum", n))
        total = total + sum_recv[n].astype(F32)
    grad_ref[...] = total.astype(BF16)
    finish()


def hand_out(head_in, grad_in, head_out, grad_out, sems):
    copies = [
        pltpu.make_async_copy(head_in, head_out, sems.at[0]),
        pltpu.make_async_copy(grad_in, grad_out, sems.at[1]),
    ]
    for copy in copies:
        copy.start()
    for copy in copies:
        copy.wait()


def on_device(
    features, point_weight, dilated_weight, branch_bias, project_weight, project_bias, cotangent
):
    in_place = pl.BlockSpec(memory_space=pltpu.HBM)
    vmem = pl.BlockSpec(memory_space=pltpu.VMEM)
    dma = pltpu.SemaphoreType.DMA
    head, grad = pl.pallas_call(
        kernel,
        out_shape=(
            pltpu.VMEM((HEIGHT, OWN, BREADTH), BF16),
            pltpu.VMEM((PIXELS, BLOCK), BF16),
        ),
        in_specs=[in_place] * 7,
        out_specs=(vmem, vmem),
        scratch_shapes=[
            pltpu.VMEM((4, OWN), F32),
            pltpu.VMEM((1, OUTPUTS), F32),
            pltpu.VMEM((LANES, CHANNELS), BF16),
            pltpu.VMEM((TERMS, CHANNELS), BF16),
            pltpu.VMEM((2 * TERMS, CHANNELS // 2), BF16),
            pltpu.VMEM((MEMBERS, 4, OWN, OUTPUTS), BF16),
            pltpu.VMEM((OUTPUTS, MEMBERS * 4 * OWN), BF16),
            pltpu.VMEM((LANES, OUTPUTS), BF16),
            pltpu.VMEM((OUTPUTS, LANES), F32),
            pltpu.VMEM((OUTPUTS, BLOCK), F32),
            pltpu.VMEM((TERMS, LANES), F32),
            pltpu.VMEM((6, OWN, LANES), F32),
            pltpu.VMEM((6, OWN, LANES), F32),
            pltpu.VMEM((MEMBERS, 4 * OWN, LANES), BF16),
            pltpu.VMEM((OUTPUTS, LANES), F32),
            pltpu.VMEM((4, 2 * OWN, LANES), BF16),
            pltpu.VMEM((6, 2 * OWN, LANES), BF16),
            pltpu.VMEM((2 * TERMS, LANES), BF16),
            pltpu.VMEM((LANES, 2 * TERMS), BF16),
            pltpu.VMEM((4, 2, PIXELS, BLOCK), F32),
            pltpu.VMEM((4, 2, PIXELS, BLOCK), BF16),
            pltpu.VMEM((4, PIXELS, BLOCK), BF16),
            pltpu.VMEM((3, PIXELS, BLOCK), BF16),
            pltpu.VMEM((3, PIXELS, BLOCK), BF16),
            pltpu.SemaphoreType.REGULAR((1,)),
            dma((13,)), dma((4,)), dma((6,)), dma((6,)), dma((23,)), dma((16, 2)),
            dma((2,)), dma((2,)), dma((3,)), dma((3,)), dma((12,)), dma((12,)),
            dma((6,)), dma((6,)), dma((4,)), dma((4,)), dma((3,)), dma((3,)),
        ],
        compiler_params=pltpu.CompilerParams(
            collective_id=0, has_side_effects=True, vmem_limit_bytes=58 * 1024 * 1024
        ),
        name="pyramid",
    )(
        features.reshape(PIXELS, CHANNELS),
        jnp.transpose(dilated_weight, (0, 1, 2, 4, 3)).reshape(TERMS - OWN, CHANNELS),
        point_weight.T,
        project_weight.reshape(4, MEMBERS, OWN, OUTPUTS),
        cotangent.reshape(PIXELS, OUTPUTS),
        branch_bias,
        project_bias.reshape(1, OUTPUTS),
    )
    head, grad = pl.pallas_call(
        hand_out,
        out_shape=(
            jax.ShapeDtypeStruct((HEIGHT, OWN, BREADTH), BF16),
            jax.ShapeDtypeStruct((PIXELS, BLOCK), BF16),
        ),
        in_specs=[vmem] * 2,
        out_specs=(in_place, in_place),
        scratch_shapes=[dma((2,))],
        name="hand_out",
    )(*[pltpu.with_memory_space_constraint(value, pltpu.VMEM) for value in (head, grad)])
    return (jnp.transpose(head, (0, 2, 1)), grad.reshape(HEIGHT, BREADTH, BLOCK))


def solution(mesh):
    in_specs = (
        P("rows", None, None),
        P(None, "filt"),
        P(None, None, None, None, "filt"),
        P(None, "filt"),
        P(),
        P(),
        P("rows", None, None),
    )
    out_specs = (P("rows", None, "filt"), P("rows", None, "filt"))
    return jax.shard_map(
        on_device, mesh=mesh, in_specs=in_specs, out_specs=out_specs, check_vma=False
    )
```
